512 devices in a mesh: cfg: 2 (over core), blk: 64 (over z, x), req: 4 (over y).
Axes of the slice: x: 4, y: 4, z: 16, core: 2. Of those that a mesh axis runs over, the one named last changes fastest.
Arguments:
- residual: bfloat16 [2, 16, 2048], P('cfg'), may hold values from -6 to 6
- queries: bfloat16 [2, 16, 4096], P('cfg', 'req'), may hold values from -80 to 80
- new_entries: bfloat16 [2, 16, 2, 2048], P('cfg', 'req'), may hold values from -6 to 6
- key_cache: bfloat16 [2, 16, 3072, 2048], P('cfg', 'req', 'blk'), may hold values from -6 to 6
- value_cache: bfloat16 [2, 16, 3072, 2048], P('cfg', 'req', 'blk'), may hold values from -8 to 8
- lengths: int32 [2, 16], P('cfg', 'req'), may hold values from 2 to 3072, as said below
- attention_ids: int32 [16, 2], replicated, may hold values from 0 to 7, all different within a row
- expert_ids: int32 [16, 2], replicated, may hold values from 0 to 7, all different within a row
- attention_router: bfloat16 [2048, 8], replicated, may hold values from -0.125 to 0.125
- expert_router: bfloat16 [2048, 8], replicated, may hold values from -0.125 to 0.125
- attention_output: bfloat16 [16384, 2048], P(('blk', 'req')), may hold values from -0.125 to 0.125
- expert_gain: bfloat16 [2048], replicated, may hold values from 0.25 to 1.75
- expert_gate: bfloat16 [45056, 2048], P(('blk', 'req')), may hold values from -0.125 to 0.125
- expert_up: bfloat16 [45056, 2048], P(('blk', 'req')), may hold values from -0.125 to 0.125
- expert_down: bfloat16 [45056, 2048], P(('blk', 'req')), may hold values from -0.078125 to 0.078125
- final_gain: bfloat16 [2048], replicated, may hold values from 0.25 to 1.75
- unembedding: bfloat16 [32000, 2048], P(('blk', 'req')), may hold values from -0.125 to 0.125
- tenant_sizes: int32 [4], replicated, may hold values from 1 to 8, 16 in all
- guidance: int32 [4], replicated, may hold values from 2 to 16
Outputs:
- guided: float32 [16, 32000], P('cfg', ('blk', 'req'))
The draws below stay inside these ranges and needn't reach their ends.
Inputs may be any that keep to these rules, and one draw needn't show every extreme that they name: lengths[0, i] lies from 1536 to 3072 and lengths[0, 0] = 3072; lengths[1, i] lies from 2 to 768 and lengths[1, 0] = 768. `tenant_sizes`: the sizes sum to 16; the largest is exactly 8. `attention_ids`: the ids of one request differ. `expert_ids`: the ids of one request differ.
All inputs are finite; a program needn't handle non-finite values.
Results may differ from the reference program's by a relative error of at most 0.017.
Values may be sent and summed in bfloat16 or wider, within the bound.
No kernel may reach another device: no remote copies, remote signals or barrier semaphores. Data moves between devices by JAX's collectives and lax.ppermute only.
A program may use at most 64 MiB of HBM per device.

```python
import math
import jax
import jax.numpy as jnp
import numpy as np
from jax import lax

D = 2048
H = 16
HD = 128
EA = 8
EM = 8
FF = 5632
V = 32000
TOPK = 2
TENANTS = 4
REQUESTS = 16
CAP = 3072


def first_keys(key):
    sub_key = jax.random.fold_in(key, 101)
    shape = (2, REQUESTS, H, HD)
    return jnp.clip(jax.random.normal(sub_key, shape, jnp.float32), -6.0, 6.0)


def draw_key_cache(key, part):
    first = first_keys(key)
    second_key = jax.random.fold_in(key, 102)
    rest_key = jax.random.fold_in(key, 103)
    rest_shape = (2, REQUESTS, CAP - 2, H, HD)
    second = jnp.clip(jax.random.normal(second_key, first.shape, jnp.float32), -6.0, 6.0)
    rest = jnp.clip(jax.random.normal(rest_key, rest_shape, jnp.float32), -6.0, 6.0)
    whole = jnp.concatenate([first[:, :, None], second[:, :, None], rest], axis=2)
    return whole.reshape(2, REQUESTS, CAP, H * HD).astype(jnp.bfloat16)


def draw_value_cache(key, part):
    noise_key = jax.random.fold_in(key, 111)
    offset_key = jax.random.fold_in(key, 112)
    shape = (2, REQUESTS, CAP, H * HD)
    place = jnp.arange(CAP).astype(jnp.float32) / CAP
    noise = jnp.clip(jax.random.normal(noise_key, shape, jnp.float32), -5.0, 5.0)
    offset = jax.random.uniform(offset_key, (2, REQUESTS, 1, H * HD), jnp.float32, -1.5, 1.5)
    ramp = 0.5 + 1.5 * place
    whole = noise + offset * ramp[None, None, :, None]
    return whole.astype(jnp.bfloat16)


def draw_queries(key, part):
    sub_key = jax.random.fold_in(key, 105)
    whole = jnp.clip(jax.random.normal(sub_key, (2, REQUESTS, TOPK, H, HD), jnp.float32), -5.0, 5.0)
    return whole.reshape(2, REQUESTS, TOPK * H * HD).astype(jnp.bfloat16)


def draw_lengths(key, part):
    cond_key = jax.random.fold_in(key, 106)
    uncond_key = jax.random.fold_in(key, 107)
    conditional = jax.random.randint(cond_key, (REQUESTS,), CAP // 2, CAP + 1).astype(jnp.int32)
    conditional = conditional.at[0].set(CAP)
    unconditional = jax.random.randint(uncond_key, (REQUESTS,), 2, CAP // 4 + 1).astype(jnp.int32)
    unconditional = unconditional.at[0].set(CAP // 4)
    return jnp.stack([conditional, unconditional]).astype(jnp.int32)


def touch_ends(array, stream_key, least, high):
    extent = array.shape
    spot = [jax.random.randint(jax.random.fold_in(stream_key, axis), (), 0, extent[axis]) for axis in range(len(extent))]
    array = array.at[tuple(spot)].set(least)
    longest = extent.index(max(extent))
    spot[longest] = (spot[longest] + 1) % extent[longest]
    return array.at[tuple(spot)].set(high)


def shard_levels(key, dims, shards, low, top_value):
    gain, own = 1.0, jax.random.fold_in(key, 6)
    for dim, shards_of in shards:
        draws = jnp.exp(jax.random.uniform(jax.random.fold_in(own, dim), (shards_of,), jnp.float32, low / len(shards), top_value / len(shards)))
        gain = gain * jnp.repeat(draws, dims[dim] // shards_of).reshape([-1 if axis == dim else 1 for axis in range(len(dims))])
    return gain


def picks_of(stream_key, rows, number_of, top, lift):
    order = jax.random.permutation(jax.random.fold_in(stream_key, 1), number_of)
    boost = order
    for power in range(3):
        boost = boost * boost // number_of
    boost = boost * lift // number_of
    tickets = jax.random.randint(jax.random.fold_in(stream_key, 2), (rows, number_of), 0, 4096) + boost
    holders = jax.random.permutation(jax.random.fold_in(stream_key, 3), rows)[jnp.arange(number_of) % rows]
    tickets = jnp.where(jnp.arange(rows)[:, None] == holders[None, :], 1 << 14, tickets)
    merit = tickets * number_of + jnp.arange(number_of)
    return lax.top_k(merit.astype(jnp.int32), top)[1].astype(jnp.int32)


def split_up(number_of, total, reach, slope):
    portions = [(1 << 20) // math.isqrt(rank ** slope) + 1 for rank in range(2, number_of + 1)]
    spare, counts = total - reach - (number_of - 1), [1] * (number_of - 1)
    while spare > 0:
        free = [i for i in range(number_of - 1) if counts[i] < reach]
        pool, budget = sum([portions[i] for i in free]), spare
        for i in free:
            more = min(reach - counts[i], max(1, budget * portions[i] // pool), spare)
            counts[i] = counts[i] + more
            spare = spare - more
    return np.array([reach] + counts)


def ragged_sizes(rng, amount, total, reach, lean):
    if amount == 2:
        one = jax.random.randint(rng, (), max(1, total - reach), min(reach, total - 1) + 1)
        return jnp.stack([one, total - one])
    sizes = jnp.asarray(split_up(amount, total, reach, lean), jnp.int32)
    twos = (amount - 1) // 2
    giver, receiver = sizes[1:1 + 2 * twos:2], sizes[2:2 + 2 * twos:2]
    margin = jnp.minimum(giver - 1, reach - receiver)
    passed = jax.random.randint(jax.random.fold_in(rng, 1), (twos,), 0, 1 << 20) % (margin + 1)
    sizes = sizes.at[1:1 + 2 * twos:2].set(giver - passed).at[2:2 + 2 * twos:2].set(receiver + passed)
    return sizes[jax.random.permutation(jax.random.fold_in(rng, 2), amount)]


def scatter_about(stream_key, extent, scale, most, split=(), dtype=jnp.bfloat16):
    values = jax.random.normal(stream_key, extent, jnp.float32) * scale
    if len(split) > 0:
        values = shard_levels(stream_key, extent, split, -0.22, 0.18) * values
    return jnp.clip(values, min=-most, max=most).astype(dtype)


def setup_inputs(seed: int = 0) -> dict:
    streams_of = jax.random.split(jax.random.key(seed), 20)
    residual = scatter_about(streams_of[0], (2, REQUESTS, D), 1.0, 6.0, ((0, 2),))
    queries = draw_queries(jax.random.fold_in(streams_of[19], 71), 0)
    new_entries = scatter_about(streams_of[2], (2, REQUESTS, 2, H * HD), 1.0, 6.0, ((0, 2), (1, 4)))
    key_cache = draw_key_cache(jax.random.fold_in(streams_of[19], 71), 0)
    value_cache = draw_value_cache(jax.random.fold_in(streams_of[19], 71), 0)
    lengths = draw_lengths(jax.random.fold_in(streams_of[19], 71), 0)
    attention_ids = picks_of(streams_of[6], REQUESTS, EA, TOPK, 2048)
    expert_ids = picks_of(streams_of[7], REQUESTS, EM, TOPK, 2048)
    attention_router = scatter_about(streams_of[8], (D, EA), D ** -0.5, 0.125)
    expert_router = scatter_about(streams_of[9], (D, EM), D ** -0.5, 0.125)
    attention_output = scatter_about(streams_of[10], (EA * H * HD, D), (H * HD) ** -0.5, 0.125, ((0, 256),))
    expert_gain = jnp.clip(1.0 + 0.15 * jax.random.normal(streams_of[11], (D,), jnp.float32), 0.25, 1.75).astype(jnp.bfloat16)
    expert_gate = scatter_about(streams_of[12], (EM * FF, D), D ** -0.5, 0.125, ((0, 256),))
    expert_up = scatter_about(streams_of[13], (EM * FF, D), D ** -0.5, 0.125, ((0, 256),))
    expert_down = scatter_about(streams_of[14], (EM * FF, D), FF ** -0.5, 0.078125, ((0, 256),))
    final_gain = jnp.clip(1.0 + 0.15 * jax.random.normal(streams_of[15], (D,), jnp.float32), 0.25, 1.75).astype(jnp.bfloat16)
    unembedding = scatter_about(streams_of[16], (V, D), D ** -0.5, 0.125, ((0, 256),))
    tenant_sizes = ragged_sizes(streams_of[17], TENANTS, REQUESTS, REQUESTS // 2, 2).astype(jnp.int32)
    guidance = touch_ends(jax.random.randint(streams_of[18], (TENANTS,), 2, 17), jax.random.fold_in(streams_of[18], 1), 2, 16).astype(jnp.int32)
    return {"residual": residual, "queries": queries, "new_entries": new_entries, "key_cache": key_cache, "value_cache": value_cache, "lengths": lengths, "attention_ids": attention_ids, "expert_ids": expert_ids, "attention_router": attention_router, "expert_router": expert_router, "attention_output": attention_output, "expert_gain": expert_gain, "expert_gate": expert_gate, "expert_up": expert_up, "expert_down": expert_down, "final_gain": final_gain, "unembedding": unembedding, "tenant_sizes": tenant_sizes, "guidance": guidance}


EPS = 1e-05

def rms_scale(values):
    return values * lax.rsqrt(lax.optimization_barrier(jnp.mean(values * values, axis=-1, keepdims=True)) + EPS)

def pair_gates(logits, chosen_ids):
    experts = jnp.arange(logits.shape[-1])
    picked = lax.optimization_barrier(jnp.sum(jnp.where(chosen_ids[:, :, None] == experts[None, None, :], logits[:, None, :], 0.0), axis=-1))
    first = jax.nn.sigmoid(picked[:, 0] - picked[:, 1])
    second = jax.nn.sigmoid(picked[:, 1] - picked[:, 0])
    return jnp.stack([first, second], axis=1)

def attend_one(operands):
    query_row, key_rows, value_rows, entries, length = operands
    factor = 1.0 / math.sqrt(HD)
    query_heads = query_row.reshape(TOPK, H, HD).astype(jnp.float32)
    key_heads = key_rows.reshape(CAP, H, HD).astype(jnp.float32)
    value_heads = value_rows.reshape(CAP, H, HD).astype(jnp.float32)
    new_key = entries[0].reshape(H, HD).astype(jnp.float32)
    new_value = entries[1].reshape(H, HD).astype(jnp.float32)
    scores = jnp.einsum('khd,phd->khp', query_heads, key_heads) * factor
    new_score = jnp.einsum('khd,hd->kh', query_heads, new_key) * factor
    live = (jnp.arange(CAP) < length)[None, None, :]
    masked = jnp.where(live, scores, -jnp.inf)
    highest = jnp.maximum(lax.optimization_barrier(jnp.max(masked, axis=-1)), new_score)
    weights = jnp.where(live, jnp.exp(masked - highest[:, :, None]), 0.0)
    new_weight = jnp.exp(new_score - highest)
    denominator = lax.optimization_barrier(jnp.sum(weights, axis=-1)) + new_weight
    rounded = lax.optimization_barrier(weights.astype(jnp.bfloat16)).astype(jnp.float32)
    new_rounded = lax.optimization_barrier(new_weight.astype(jnp.bfloat16)).astype(jnp.float32)
    numerator = jnp.einsum('khp,phd->khd', rounded, value_heads) + new_rounded[:, :, None] * new_value[None, :, :]
    return (numerator / denominator[:, :, None]).astype(jnp.bfloat16).reshape(TOPK, H * HD)

def reference(residual, queries, new_entries, key_cache, value_cache, lengths, attention_ids, expert_ids, attention_router, expert_router, attention_output, expert_gain, expert_gate, expert_up, expert_down, final_gain, unembedding, tenant_sizes, guidance):
    total_rows = 2 * REQUESTS
    attention_out = lax.map(attend_one, (queries.reshape(total_rows, TOPK * H * HD), key_cache.reshape(total_rows, CAP, H * HD), value_cache.reshape(total_rows, CAP, H * HD), new_entries.reshape(total_rows, 2, H * HD), lengths.reshape(total_rows)))
    inputs = residual.reshape(total_rows, D).astype(jnp.float32)
    normed_input = rms_scale(inputs).astype(jnp.bfloat16)
    attention_both = jnp.concatenate([attention_ids, attention_ids], axis=0)
    expert_both = jnp.concatenate([expert_ids, expert_ids], axis=0)
    attention_gates = pair_gates(jnp.dot(normed_input, attention_router, preferred_element_type=jnp.float32), attention_both)
    gated_out = (attention_gates[:, :, None] * attention_out.astype(jnp.float32)).astype(jnp.bfloat16)
    attention_onehot = (attention_both[:, :, None] == jnp.arange(EA)[None, None, :]).astype(jnp.float32)
    placed = jnp.einsum('rke,rkf->ref', attention_onehot, gated_out.astype(jnp.float32)).astype(jnp.bfloat16)
    attention_proj = jnp.dot(placed.reshape(total_rows, EA * H * HD), attention_output, preferred_element_type=jnp.float32)
    middle = inputs + attention_proj
    expert_input = (rms_scale(middle) * expert_gain.astype(jnp.float32)).astype(jnp.bfloat16)
    expert_gates = pair_gates(jnp.dot(expert_input, expert_router, preferred_element_type=jnp.float32), expert_both)
    expert_onehot = (expert_both[:, :, None] == jnp.arange(EM)[None, None, :]).astype(jnp.float32)
    expert_share = jnp.einsum('rke,rk->re', expert_onehot, expert_gates)
    spread = jnp.repeat(expert_share, FF, axis=1)
    gate_values = jnp.dot(expert_input, expert_gate.T, preferred_element_type=jnp.float32)
    up_values = jnp.dot(expert_input, expert_up.T, preferred_element_type=jnp.float32)
    expert_hidden = (jax.nn.silu(gate_values) * up_values * spread).astype(jnp.bfloat16)
    expert_out = jnp.dot(expert_hidden, expert_down, preferred_element_type=jnp.float32)
    final_input = (rms_scale(middle + expert_out) * final_gain.astype(jnp.float32)).astype(jnp.bfloat16)
    logits = jnp.dot(final_input, unembedding.T, preferred_element_type=jnp.float32).reshape(2, REQUESTS, V)
    request_index = jnp.arange(REQUESTS).astype(jnp.int32)
    tenant_ends = jnp.cumsum(tenant_sizes).astype(jnp.int32)
    tenant = lax.optimization_barrier(jnp.sum((request_index[:, None] >= tenant_ends[None, :]).astype(jnp.int32), axis=1))
    tenant_onehot = tenant[:, None] == jnp.arange(TENANTS)[None, :]
    factor = lax.optimization_barrier(jnp.sum(jnp.where(tenant_onehot, guidance[None, :], 0), axis=1)).astype(jnp.float32) / 4.0
    return logits[1] + factor[:, None] * (logits[0] - logits[1])
```

```python
import math

import jax
import jax.numpy as jnp
from jax import lax
from jax.experimental import pallas as pl
from jax.experimental.pallas import tpu as pltpu
from jax.sharding import Mesh
from jax.sharding import PartitionSpec as P

D = 2048
H = 16
HD = 128
FF = 5632
TOPK = 2
EPS = 1e-05
NEG = -1e30
LANES = 128
HEADS_ROW = 4
ROW = HEADS_ROW * HD + LANES
SCALE = 1.0 / math.sqrt(HD)

F32 = jnp.float32
BF16 = jnp.bfloat16
NT = (((1,), (1,)), ((), ()))


def vmem():
    return pl.BlockSpec(memory_space=pltpu.VMEM)


def smem():
    return pl.BlockSpec(memory_space=pltpu.SMEM)


def call(body, outs, specs, scratch=()):
    return pl.pallas_call(
        body,
        out_shape=outs,
        in_specs=specs,
        out_specs=jax.tree.map(lambda _: vmem(), outs),
        scratch_shapes=list(scratch),
        compiler_params=pltpu.CompilerParams(vmem_limit_bytes=48 * 1024 * 1024),
    )


def iota(shape, dim):
    return lax.broadcasted_iota(jnp.int32, shape, dim)


def dot(a, b):
    return jnp.dot(a, b, preferred_element_type=F32)


def rms(values):
    return lax.rsqrt(jnp.mean(values * values, axis=-1, keepdims=True) + EPS)


def expert_of_plane():
    return lax.axis_index("z") // 2


def share_column(logits_t, ids_ref, expert, lane_of_row):
    experts = iota(logits_t.shape, 0)
    first_id, second_id = ids_ref[0:1, :], ids_ref[1:2, :]
    first = jnp.sum(jnp.where(experts == first_id, logits_t, 0.0), axis=0, keepdims=True)
    second = jnp.sum(jnp.where(experts == second_id, logits_t, 0.0), axis=0, keepdims=True)
    gate_first = 1.0 / (1.0 + jnp.exp(second - first))
    gate_second = 1.0 / (1.0 + jnp.exp(first - second))
    share = jnp.where(first_id == expert, gate_first, 0.0) + jnp.where(
        second_id == expert, gate_second, 0.0
    )
    lanes = iota((lane_of_row.shape[0], share.shape[1]), 1)
    return jnp.sum(jnp.where(lanes == lane_of_row, share, 0.0), axis=1, keepdims=True)


def attend_kernel(
    q_ref, k_ref, v_ref, new_ref, lengths_ref, ids_ref, out_ref, rows_ref
):
    requests, positions = k_ref.shape[1], k_ref.shape[2]
    block = lax.axis_index("z") * lax.axis_size("x") + lax.axis_index("x")
    first_request = lax.axis_index("req") * requests
    queries = q_ref[0].astype(F32)
    own_head = iota((H, D), 0) == iota((H, D), 1) // HD
    place = block * positions + iota((1, positions), 1)
    sub = iota((8, LANES), 0)
    lane = iota((8, LANES), 1)
    for r in range(requests):
        wide = jnp.concatenate(
            [
                jnp.where(own_head, queries[r : r + 1, k * D : (k + 1) * D], 0.0)
                for k in range(TOPK)
            ],
            axis=0,
        )
        scores = (
            lax.dot_general(wide.astype(BF16), k_ref[0, r], NT, preferred_element_type=F32) * SCALE
        )
        entry = new_ref[0, r].astype(F32)
        new_score = jnp.sum(wide * entry[0:1, :], axis=1, keepdims=True) * SCALE
        live = place < lengths_ref[0, r]
        owner = block == 0
        top = jnp.max(jnp.where(live, scores, NEG), axis=1, keepdims=True)
        top = jnp.maximum(top, jnp.where(owner, new_score, NEG))
        peak = top.astype(BF16).astype(F32)
        weights = jnp.where(live, jnp.exp(scores - peak), 0.0)
        fresh = jnp.where(owner, jnp.exp(new_score - peak), 0.0)
        total = jnp.sum(weights, axis=1, keepdims=True) + fresh
        high = total.astype(BF16).astype(F32)
        low = total - high
        values = dot(weights.astype(BF16), v_ref[0, r])
        values = values + fresh.astype(BF16).astype(F32) * entry[1:2, :]
        for k in range(TOPK):
            for quarter in range(H // HEADS_ROW):
                half, group = quarter // 2, quarter % 2
                base = k * H + (quarter // 2) * 8
                parts = []
                for j in range(HEADS_ROW):
                    head = quarter * HEADS_ROW + j
                    tile = values[base : base + 8, head * HD : (head + 1) * HD]
                    parts.append(jnp.sum(jnp.where(sub == head % 8, tile, 0.0), axis=0, keepdims=True))
                column = sub - group * HEADS_ROW
                here = (column >= 0) & (column < HEADS_ROW)
                stats = jnp.where(lane == column, peak[base : base + 8], 0.0)
                stats = stats + jnp.where(lane == column + 4, high[base : base + 8], 0.0)
                stats = stats + jnp.where(lane == column + 8, low[base : base + 8], 0.0)
                parts.append(jnp.sum(jnp.where(here, stats, 0.0), axis=0, keepdims=True))
                row = group * requests + r
                rows_ref[half, k, row : row + 1, :] = jnp.concatenate(parts, axis=1)
    request = iota((8, 1), 0) % requests
    chosen = []
    for k in range(TOPK):
        picked = jnp.zeros((8, 1), jnp.int32)
        for r in range(requests):
            picked = jnp.where(request == r, ids_ref[first_request + r, k], picked)
        chosen.append(picked)
    for plane in range(out_ref.shape[0]):
        expert, half = plane // 2, plane % 2
        message = jnp.where(chosen[0] == expert, rows_ref[half, 0], 0.0)
        message = message + jnp.where(chosen[1] == expert, rows_ref[half, 1], 0.0)
        out_ref[plane] = message.astype(BF16)


def spread_lanes(first_lane):
    rows, columns = iota((LANES, HEADS_ROW * HD), 0), iota((LANES, HEADS_ROW * HD), 1)
    return rows == first_lane + columns // HD


def merged(parts, stats, groups):
    count = stats.shape[0]
    peak = jnp.max(stats, axis=0)
    scale = jnp.exp(stats - peak[None])
    rows = count * groups * 8
    flat = scale.reshape(rows, LANES)
    high = flat.astype(BF16)
    low = (flat - high.astype(F32)).astype(BF16)
    lift = spread_lanes(0).astype(BF16)
    scales = dot(high, lift) + dot(low, lift)
    sums = dot(
        stats.reshape(rows, LANES).astype(BF16), (spread_lanes(4) | spread_lanes(8)).astype(BF16)
    )
    numerator, denominator = [], []
    for g in range(groups):
        top, bottom = 0.0, 0.0
        for n in range(count):
            at = (n * groups + g) * 8
            factor = scales[at : at + 8]
            top = top + parts(n, g) * factor
            bottom = bottom + sums[at : at + 8] * factor
        numerator.append(top)
        denominator.append(bottom)
    return numerator, denominator, peak


def merge_kernel(in_ref, weight_ref, out_ref):
    wide = HEADS_ROW * HD
    copies = out_ref.shape[0]
    stats = in_ref[:, :, wide:].astype(F32)[:, None]
    numerator, denominator, peak = merged(
        lambda n, g: in_ref[n, :, :wide].astype(F32), stats, 1
    )
    lane = iota((8, LANES), 1)
    packed = jnp.where(lane < HEADS_ROW, peak[0], 0.0)
    for j in range(HEADS_ROW):
        total = denominator[0][:, j * HD : (j + 1) * HD]
        high = total.astype(BF16).astype(F32)
        packed = jnp.where(lane == 4 + j, high, packed)
        packed = jnp.where(lane == 8 + j, total - high, packed)
    blocks = [numerator[0][:, j * HD : (j + 1) * HD] for j in range(HEADS_ROW)] + [packed]
    blocks = [block.astype(BF16) for block in blocks]
    for copy in range(copies):
        for j, block in enumerate(blocks):
            out_ref[copy, j * 8 : (j + 1) * 8, :] = block
        out_ref[copy, len(blocks) * 8 :, :] = weight_ref[:, copy * LANES : (copy + 1) * LANES]


def project_kernel(in_ref, residual_ref, router_ref, ids_ref, out_ref, stats_ref, weight_ref):
    requests = 4
    columns, groups = 4, 4
    head_rows = HEADS_ROW * 8
    weight_rows = in_ref.shape[1] - head_rows - 8
    sources = in_ref.shape[0]
    expert = expert_of_plane()
    for source in range(sources):
        stats_ref[source] = in_ref[source, head_rows : head_rows + 8, :].astype(F32)
        weight_ref[source * weight_rows : (source + 1) * weight_rows, :] = in_ref[
            source, head_rows + 8 :, :
        ]
    stats = stats_ref[...].reshape(columns, groups, 8, LANES)

    def part(n, g):
        source = n * groups + g
        return jnp.concatenate(
            [in_ref[source, j * 8 : (j + 1) * 8, :] for j in range(HEADS_ROW)], axis=1
        ).astype(F32)

    numerator, denominator, _ = merged(part, stats, groups)
    inputs = residual_ref[0].astype(F32)
    normed = (inputs * rms(inputs)).astype(BF16)
    logits = lax.dot_general(router_ref[...], normed, NT, preferred_element_type=F32)
    row = iota((8 * groups, 1), 0)
    gate = share_column(logits, ids_ref, expert, row // 8 * requests + row % requests)
    attended = jnp.concatenate(
        [top / jnp.maximum(bottom, 1e-30) for top, bottom in zip(numerator, denominator)], axis=0
    )
    gated = (attended.astype(BF16).astype(F32) * gate).astype(BF16)
    wide = HEADS_ROW * HD
    lower = dot(gated, weight_ref[:wide, :])
    upper = dot(gated, weight_ref[wide:, :])
    mixed = jnp.where(row % 8 < requests, lower, upper)
    sub = iota((8, LANES), 0)
    tiles = []
    for g in range(groups):
        tile = mixed[g * 8 : (g + 1) * 8]
        tiles.append(tile + pltpu.roll(tile, 4, 0))
    for pair in range(groups // 2):
        both = jnp.where(sub < requests, tiles[2 * pair], tiles[2 * pair + 1]).astype(BF16)
        for copy in range(out_ref.shape[0]):
            out_ref[copy, pair * 8 : (pair + 1) * 8, :] = both


def fold_kernel(in_ref, out_ref):
    total = in_ref[0].astype(F32)
    for n in range(1, in_ref.shape[0]):
        total = total + in_ref[n].astype(F32)
    total = total.astype(BF16)
    for copy in range(out_ref.shape[0]):
        out_ref[copy] = total


def expert_kernel(
    in_ref, residual_ref, gain_ref, router_ref, ids_ref, gate_ref, up_ref, down_ref, out_ref, middle_ref
):
    chunks = in_ref.shape[0]
    requests = in_ref.shape[1]
    for chunk in range(chunks):
        at = slice(chunk * LANES, (chunk + 1) * LANES)
        middle_ref[:, at] = residual_ref[0, :, at].astype(F32) + in_ref[chunk].astype(F32)
    middle = middle_ref[...]
    inputs = (middle * rms(middle) * gain_ref[...].astype(F32)).astype(BF16)
    logits = lax.dot_general(router_ref[...], inputs, NT, preferred_element_type=F32)
    share = share_column(logits, ids_ref, expert_of_plane(), iota((requests, 1), 0))
    gate = lax.dot_general(inputs, gate_ref[...], NT, preferred_element_type=F32)
    up = lax.dot_general(inputs, up_ref[...], NT, preferred_element_type=F32)
    hidden = (gate / (1.0 + jnp.exp(-gate)) * up * share).astype(BF16)
    for chunk in range(chunks):
        at = slice(chunk * LANES, (chunk + 1) * LANES)
        out_ref[chunk] = dot(hidden, down_ref[:, at]).astype(BF16)


def finish_kernel(in_ref, attention_ref, residual_ref, out_ref):
    total = attention_ref[0].astype(F32)
    for n in range(1, attention_ref.shape[0]):
        total = total + attention_ref[n].astype(F32)
    for n in range(in_ref.shape[0]):
        total = total + in_ref[n].astype(F32)
    chunk = lax.axis_index("x") * lax.axis_size("req") + lax.axis_index("req")
    at = pl.ds(pl.multiple_of(chunk * LANES, LANES), LANES)
    total = (total + residual_ref[0, :, at].astype(F32)).astype(out_ref.dtype)
    half = out_ref.shape[1]
    copies = out_ref.shape[0] // 2
    for stream in range(2):
        for copy in range(copies):
            out_ref[stream * copies + copy] = total[stream * half : (stream + 1) * half]


def head_kernel(in_ref, gain_ref, words_ref, sizes_ref, guidance_ref, out_ref, joined_ref):
    half = in_ref.shape[1]
    chunks = in_ref.shape[0] // 2
    for stream in range(2):
        for chunk in range(chunks):
            at = slice(chunk * LANES, (chunk + 1) * LANES)
            joined_ref[stream * half : (stream + 1) * half, at] = in_ref[
                stream * chunks + chunk
            ].astype(F32)
    joined = joined_ref[...]
    inputs = (joined * rms(joined) * gain_ref[...].astype(F32)).astype(BF16)
    logits = lax.dot_general(inputs, words_ref[...], NT, preferred_element_type=F32)
    request = lax.axis_index("cfg") * half + iota((half, 1), 0)
    tenants = sizes_ref.shape[0]
    tenant = jnp.zeros((half, 1), jnp.int32)
    end = 0
    for t in range(tenants):
        end = end + sizes_ref[t]
        tenant = tenant + (request >= end).astype(jnp.int32)
    chosen = jnp.zeros((half, 1), jnp.int32)
    for t in range(tenants):
        chosen = jnp.where(tenant == t, guidance_ref[t], chosen)
    factor = chosen.astype(F32) / 4.0
    conditional, unconditional = logits[:half], logits[half:]
    out_ref[...] = unconditional + factor * (conditional - unconditional)


def exchanged(value, axis):
    return lax.all_to_all(value, axis, 0, 0, tiled=True)


def local(
    residual,
    queries,
    new_entries,
    key_cache,
    value_cache,
    lengths,
    attention_ids,
    expert_ids,
    attention_router,
    expert_router,
    attention_output,
    expert_gain,
    expert_gate,
    expert_up,
    expert_down,
    final_gain,
    unembedding,
    tenant_sizes,
    guidance,
):
    planes = lax.axis_size("z")
    plane = ("x", "req")
    members = lax.axis_size(plane)
    requests = residual.shape[1]
    shape = jax.ShapeDtypeStruct

    partial = call(
        attend_kernel,
        shape((planes, 8, ROW), BF16),
        [vmem()] * 4 + [smem()] * 2,
        [pltpu.VMEM((2, TOPK, 8, ROW), F32)],
    )(queries, key_cache, value_cache, new_entries, lengths, attention_ids)
    partial = exchanged(partial, "z")

    weight_rows = attention_output.shape[0]
    merged_rows = HEADS_ROW * 8 + 8 + weight_rows
    both = call(merge_kernel, shape((members, merged_rows, LANES), BF16), [vmem()] * 2)(
        partial, attention_output
    )
    both = exchanged(both, plane)

    chunk = shape((planes, requests, LANES), BF16)
    projected = call(
        project_kernel,
        chunk,
        [vmem()] * 4,
        [pltpu.VMEM((members, 8, LANES), F32), pltpu.VMEM((members * weight_rows, LANES), BF16)],
    )(both, residual, attention_router.T, attention_ids.T)
    projected = exchanged(projected, "z")

    spread = shape((members, requests, LANES), BF16)
    attention = call(fold_kernel, spread, [vmem()])(projected)
    attention = exchanged(attention, plane)

    hidden = call(
        expert_kernel, spread, [vmem()] * 8, [pltpu.VMEM((requests, D), F32)]
    )(
        attention,
        residual,
        expert_gain[None],
        expert_router.T,
        expert_ids.T,
        expert_gate,
        expert_up,
        expert_down,
    )
    hidden = exchanged(hidden, plane)
    hidden = call(fold_kernel, chunk, [vmem()])(hidden)
    hidden = exchanged(hidden, "z")

    streams = lax.axis_size("cfg")
    final = call(
        finish_kernel, shape((streams * members, requests // 2, LANES), BF16), [vmem()] * 3
    )(hidden, projected, residual)
    final = exchanged(final, ("cfg",) + plane)

    return call(
        head_kernel,
        shape((requests // 2, unembedding.shape[0]), F32),
        [vmem()] * 3 + [smem()] * 2,
        [pltpu.VMEM((requests, D), F32)],
    )(final, final_gain[None], unembedding, tenant_sizes, guidance)


def solution(mesh):
    sizes = mesh.devices.shape
    split = Mesh(mesh.devices.reshape(sizes[0], 16, sizes[1] // 16, sizes[2]), ("cfg", "z", "x", "req"))
    blk = ("z", "x")
    rows = P(("z", "x", "req"), None)
    placed = (
        P("cfg", None, None),
        P("cfg", "req", None),
        P("cfg", "req", None, None),
        P("cfg", "req", blk, None),
        P("cfg", "req", blk, None),
        P("cfg", "req"),
        P(),
        P(),
        P(),
        P(),
        rows,
        P(),
        rows,
        rows,
        rows,
        P(),
        rows,
        P(),
        P(),
    )
    return jax.shard_map(
        local,
        mesh=split,
        in_specs=placed,
        out_specs=P("cfg", ("z", "x", "req")),
        check_vma=False,
    )
```

```python
import math

import jax
import jax.numpy as jnp
from jax import lax
from jax.experimental import pallas as pl
from jax.experimental.pallas import tpu as pltpu
from jax.sharding import Mesh
from jax.sharding import PartitionSpec as P

D = 2048
H = 16
HD = 128
FF = 5632
TOPK = 2
EPS = 1e-05
NEG = -1e30
LANES = 128
HEADS_ROW = 4
ROW = HEADS_ROW * HD + LANES
SCALE = 1.0 / math.sqrt(HD)

F32 = jnp.float32
BF16 = jnp.bfloat16
NT = (((1,), (1,)), ((), ()))


def vmem():
    return pl.BlockSpec(memory_space=pltpu.VMEM)


def hbm():
    return pl.BlockSpec(memory_space=pltpu.HBM)


def call(body, outs, specs, scratch=()):
    return pl.pallas_call(
        body,
        out_shape=outs,
        in_specs=specs,
        out_specs=jax.tree.map(lambda _: vmem(), outs),
        scratch_shapes=list(scratch),
        compiler_params=pltpu.CompilerParams(vmem_limit_bytes=48 * 1024 * 1024),
    )


def iota(shape, dim):
    return lax.broadcasted_iota(jnp.int32, shape, dim)


def dot(a, b):
    return jnp.dot(a, b, preferred_element_type=F32)


def rms(values):
    return lax.rsqrt(jnp.mean(values * values, axis=-1, keepdims=True) + EPS)


def expert_of_plane():
    return lax.axis_index("z") // 2


def share_column(logits_t, ids_ref, expert, lane_of_row):
    experts = iota(logits_t.shape, 0)
    first_id, second_id = ids_ref[0:1, :], ids_ref[1:2, :]
    first = jnp.sum(jnp.where(experts == first_id, logits_t, 0.0), axis=0, keepdims=True)
    second = jnp.sum(jnp.where(experts == second_id, logits_t, 0.0), axis=0, keepdims=True)
    gate_first = 1.0 / (1.0 + jnp.exp(second - first))
    gate_second = 1.0 / (1.0 + jnp.exp(first - second))
    share = jnp.where(first_id == expert, gate_first, 0.0) + jnp.where(
        second_id == expert, gate_second, 0.0
    )
    lanes = iota((lane_of_row.shape[0], share.shape[1]), 1)
    return jnp.sum(jnp.where(lanes == lane_of_row, share, 0.0), axis=1, keepdims=True)


def guidance_factor(sizes_ref, guidance_ref, half):
    request = lax.axis_index("cfg") * half + iota((half, 1), 0)
    tenants = sizes_ref.shape[0]
    tenant = jnp.zeros((half, 1), jnp.int32)
    end = 0
    for t in range(tenants):
        end = end + sizes_ref[t]
        tenant = tenant + (request >= end).astype(jnp.int32)
    chosen = jnp.zeros((half, 1), jnp.int32)
    for t in range(tenants):
        chosen = jnp.where(tenant == t, guidance_ref[t], chosen)
    return chosen.astype(F32) / 4.0


def attend_kernel(
    q_hbm,
    k_hbm,
    v_hbm,
    new_hbm,
    lengths_hbm,
    ids_hbm,
    sizes_hbm,
    guidance_hbm,
    out_ref,
    factor_ref,
    q_ref,
    k_ref,
    v_ref,
    new_ref,
    lengths_ref,
    ids_ref,
    sizes_ref,
    guidance_ref,
    rows_ref,
    small_sems,
    key_sems,
    value_sems,
):
    requests, positions = k_ref.shape[0], k_ref.shape[1]
    small = [
        pltpu.make_async_copy(source, target, small_sems.at[n])
        for n, (source, target) in enumerate(
            [
                (q_hbm, q_ref),
                (new_hbm, new_ref),
                (lengths_hbm, lengths_ref),
                (ids_hbm, ids_ref),
                (sizes_hbm, sizes_ref),
                (guidance_hbm, guidance_ref),
            ]
        )
    ]
    keys = [
        pltpu.make_async_copy(k_hbm.at[0, r], k_ref.at[r], key_sems.at[r]) for r in range(requests)
    ]
    values_in = [
        pltpu.make_async_copy(v_hbm.at[0, r], v_ref.at[r], value_sems.at[r])
        for r in range(requests)
    ]
    for copy in small:
        copy.start()
    for key, value in zip(keys, values_in):
        key.start()
        value.start()
    for copy in small:
        copy.wait()
    factor_ref[...] = jnp.broadcast_to(
        guidance_factor(sizes_ref, guidance_ref, factor_ref.shape[0]), factor_ref.shape
    )
    block = lax.axis_index("z") * lax.axis_size("x") + lax.axis_index("x")
    first_request = lax.axis_index("req") * requests
    queries = q_ref[0].astype(F32)
    own_head = iota((H, D), 0) == iota((H, D), 1) // HD
    place = block * positions + iota((1, positions), 1)
    sub = iota((8, LANES), 0)
    lane = iota((8, LANES), 1)
    for r in range(requests):
        wide = jnp.concatenate(
            [
                jnp.where(own_head, queries[r : r + 1, k * D : (k + 1) * D], 0.0)
                for k in range(TOPK)
            ],
            axis=0,
        )
        keys[r].wait()
        scores = (
            lax.dot_general(wide.astype(BF16), k_ref[r], NT, preferred_element_type=F32) * SCALE
        )
        entry = new_ref[0, r].astype(F32)
        new_score = jnp.sum(wide * entry[0:1, :], axis=1, keepdims=True) * SCALE
        live = place < lengths_ref[0, r]
        owner = block == 0
        top = jnp.max(jnp.where(live, scores, NEG), axis=1, keepdims=True)
        top = jnp.maximum(top, jnp.where(owner, new_score, NEG))
        peak = top.astype(BF16).astype(F32)
        weights = jnp.where(live, jnp.exp(scores - peak), 0.0)
        fresh = jnp.where(owner, jnp.exp(new_score - peak), 0.0)
        total = jnp.sum(weights, axis=1, keepdims=True) + fresh
        high = total.astype(BF16).astype(F32)
        low = total - high
        values_in[r].wait()
        values = dot(weights.astype(BF16), v_ref[r])
        values = values + fresh.astype(BF16).astype(F32) * entry[1:2, :]
        for k in range(TOPK):
            for quarter in range(H // HEADS_ROW):
                half, group = quarter // 2, quarter % 2
                base = k * H + (quarter // 2) * 8
                parts = []
                for j in range(HEADS_ROW):
                    head = quarter * HEADS_ROW + j
                    tile = values[base : base + 8, head * HD : (head + 1) * HD]
                    parts.append(jnp.sum(jnp.where(sub == head % 8, tile, 0.0), axis=0, keepdims=True))
                column = sub - group * HEADS_ROW
                here = (column >= 0) & (column < HEADS_ROW)
                stats = jnp.where(lane == column, peak[base : base + 8], 0.0)
                stats = stats + jnp.where(lane == column + 4, high[base : base + 8], 0.0)
                stats = stats + jnp.where(lane == column + 8, low[base : base + 8], 0.0)
                parts.append(jnp.sum(jnp.where(here, stats, 0.0), axis=0, keepdims=True))
                row = group * requests + r
                rows_ref[half, k, row : row + 1, :] = jnp.concatenate(parts, axis=1)
    request = iota((8, 1), 0) % requests
    chosen = []
    for k in range(TOPK):
        picked = jnp.zeros((8, 1), jnp.int32)
        for r in range(requests):
            picked = jnp.where(request == r, ids_ref[k, first_request + r], picked)
        chosen.append(picked)
    for plane in range(out_ref.shape[0]):
        expert, half = plane // 2, plane % 2
        message = jnp.where(chosen[0] == expert, rows_ref[half, 0], 0.0)
        message = message + jnp.where(chosen[1] == expert, rows_ref[half, 1], 0.0)
        out_ref[plane] = message.astype(BF16)


def spread_lanes(first_lane):
    rows, columns = iota((LANES, HEADS_ROW * HD), 0), iota((LANES, HEADS_ROW * HD), 1)
    return rows == first_lane + columns // HD


def merged(parts, stats, groups):
    count = stats.shape[0]
    peak = jnp.max(stats, axis=0)
    scale = jnp.exp(stats - peak[None])
    rows = count * groups * 8
    flat = scale.reshape(rows, LANES)
    high = flat.astype(BF16)
    low = (flat - high.astype(F32)).astype(BF16)
    lift = spread_lanes(0).astype(BF16)
    scales = dot(high, lift) + dot(low, lift)
    sums = dot(
        stats.reshape(rows, LANES).astype(BF16), (spread_lanes(4) | spread_lanes(8)).astype(BF16)
    )
    numerator, denominator = [], []
    for g in range(groups):
        top, bottom = 0.0, 0.0
        for n in range(count):
            at = (n * groups + g) * 8
            factor = scales[at : at + 8]
            top = top + parts(n, g) * factor
            bottom = bottom + sums[at : at + 8] * factor
        numerator.append(top)
        denominator.append(bottom)
    return numerator, denominator, peak


def merge_kernel(
    in_ref, weight_ref, first_gain_ref, second_gain_ref, ids_ref, out_ref, gains_ref, ids_out_ref
):
    gains_ref[0, :] = first_gain_ref[...].astype(F32)
    gains_ref[1, :] = second_gain_ref[...].astype(F32)
    ids_out_ref[...] = ids_ref[...]
    wide = HEADS_ROW * HD
    copies = out_ref.shape[0]
    stats = in_ref[:, :, wide:].astype(F32)[:, None]
    numerator, denominator, peak = merged(
        lambda n, g: in_ref[n, :, :wide].astype(F32), stats, 1
    )
    lane = iota((8, LANES), 1)
    packed = jnp.where(lane < HEADS_ROW, peak[0], 0.0)
    for j in range(HEADS_ROW):
        total = denominator[0][:, j * HD : (j + 1) * HD]
        high = total.astype(BF16).astype(F32)
        packed = jnp.where(lane == 4 + j, high, packed)
        packed = jnp.where(lane == 8 + j, total - high, packed)
    blocks = [numerator[0][:, j * HD : (j + 1) * HD] for j in range(HEADS_ROW)] + [packed]
    blocks = [block.astype(BF16) for block in blocks]
    for copy in range(copies):
        for j, block in enumerate(blocks):
            out_ref[copy, j * 8 : (j + 1) * 8, :] = block
        out_ref[copy, len(blocks) * 8 :, :] = weight_ref[:, copy * LANES : (copy + 1) * LANES]


def project_kernel(in_ref, residual_ref, router_ref, ids_ref, out_ref, stats_ref, weight_ref):
    requests = 4
    columns, groups = 4, 4
    head_rows = HEADS_ROW * 8
    weight_rows = in_ref.shape[1] - head_rows - 8
    sources = in_ref.shape[0]
    expert = expert_of_plane()
    for source in range(sources):
        stats_ref[source] = in_ref[source, head_rows : head_rows + 8, :].astype(F32)
        weight_ref[source * weight_rows : (source + 1) * weight_rows, :] = in_ref[
            source, head_rows + 8 :, :
        ]
    stats = stats_ref[...].reshape(columns, groups, 8, LANES)

    def part(n, g):
        source = n * groups + g
        return jnp.concatenate(
            [in_ref[source, j * 8 : (j + 1) * 8, :] for j in range(HEADS_ROW)], axis=1
        ).astype(F32)

    numerator, denominator, _ = merged(part, stats, groups)
    inputs = residual_ref[0].astype(F32)
    normed = (inputs * rms(inputs)).astype(BF16)
    logits = lax.dot_general(router_ref[...], normed, NT, preferred_element_type=F32)
    row = iota((8 * groups, 1), 0)
    gate = share_column(logits, ids_ref, expert, row // 8 * requests + row % requests)
    attended = jnp.concatenate(
        [top / jnp.maximum(bottom, 1e-30) for top, bottom in zip(numerator, denominator)], axis=0
    )
    gated = (attended.astype(BF16).astype(F32) * gate).astype(BF16)
    wide = HEADS_ROW * HD
    lower = dot(gated, weight_ref[:wide, :])
    upper = dot(gated, weight_ref[wide:, :])
    mixed = jnp.where(row % 8 < requests, lower, upper)
    sub = iota((8, LANES), 0)
    tiles = []
    for g in range(groups):
        tile = mixed[g * 8 : (g + 1) * 8]
        tiles.append(tile + pltpu.roll(tile, 4, 0))
    for pair in range(groups // 2):
        both = jnp.where(sub < requests, tiles[2 * pair], tiles[2 * pair + 1]).astype(BF16)
        for copy in range(out_ref.shape[0]):
            out_ref[copy, pair * 8 : (pair + 1) * 8, :] = both


def fold_kernel(in_ref, out_ref):
    total = in_ref[0].astype(F32)
    for n in range(1, in_ref.shape[0]):
        total = total + in_ref[n].astype(F32)
    total = total.astype(BF16)
    for copy in range(out_ref.shape[0]):
        out_ref[copy] = total


def expert_kernel(
    in_ref, residual_ref, gain_ref, router_ref, ids_ref, gate_ref, up_ref, down_ref, out_ref, middle_ref
):
    chunks = in_ref.shape[0]
    requests = in_ref.shape[1]
    for chunk in range(chunks):
        at = slice(chunk * LANES, (chunk + 1) * LANES)
        middle_ref[:, at] = residual_ref[0, :, at].astype(F32) + in_ref[chunk].astype(F32)
    middle = middle_ref[...]
    inputs = (middle * rms(middle) * gain_ref[0:1, :]).astype(BF16)
    logits = lax.dot_general(router_ref[...], inputs, NT, preferred_element_type=F32)
    share = share_column(logits, ids_ref, expert_of_plane(), iota((requests, 1), 0))
    gate = lax.dot_general(inputs, gate_ref[...], NT, preferred_element_type=F32)
    up = lax.dot_general(inputs, up_ref[...], NT, preferred_element_type=F32)
    hidden = (gate / (1.0 + jnp.exp(-gate)) * up * share).astype(BF16)
    for chunk in range(chunks):
        at = slice(chunk * LANES, (chunk + 1) * LANES)
        out_ref[chunk] = dot(hidden, down_ref[:, at]).astype(BF16)


def finish_kernel(in_ref, attention_ref, residual_ref, out_ref):
    total = attention_ref[0].astype(F32)
    for n in range(1, attention_ref.shape[0]):
        total = total + attention_ref[n].astype(F32)
    for n in range(in_ref.shape[0]):
        total = total + in_ref[n].astype(F32)
    chunk = lax.axis_index("x") * lax.axis_size("req") + lax.axis_index("req")
    at = pl.ds(pl.multiple_of(chunk * LANES, LANES), LANES)
    total = (total + residual_ref[0, :, at].astype(F32)).astype(out_ref.dtype)
    half = out_ref.shape[1]
    copies = out_ref.shape[0] // 2
    for stream in range(2):
        for copy in range(copies):
            out_ref[stream * copies + copy] = total[stream * half : (stream + 1) * half]


def head_kernel(in_ref, gain_ref, words_ref, factor_ref, out_ref, joined_ref):
    half = in_ref.shape[1]
    chunks = in_ref.shape[0] // 2
    for stream in range(2):
        for chunk in range(chunks):
            at = slice(chunk * LANES, (chunk + 1) * LANES)
            joined_ref[stream * half : (stream + 1) * half, at] = in_ref[
                stream * chunks + chunk
            ].astype(F32)
    joined = joined_ref[...]
    inputs = (joined * rms(joined) * gain_ref[1:2, :]).astype(BF16)
    logits = lax.dot_general(inputs, words_ref[...], NT, preferred_element_type=F32)
    factor = factor_ref[:, :1]
    conditional, unconditional = logits[:half], logits[half:]
    out_ref[...] = unconditional + factor * (conditional - unconditional)


def exchanged(value, axis):
    return lax.all_to_all(value, axis, 0, 0, tiled=True)


def local(
    residual,
    queries,
    new_entries,
    key_cache,
    value_cache,
    lengths,
    attention_ids,
    expert_ids,
    attention_router,
    expert_router,
    attention_output,
    expert_gain,
    expert_gate,
    expert_up,
    expert_down,
    final_gain,
    unembedding,
    tenant_sizes,
    guidance,
):
    planes = lax.axis_size("z")
    plane = ("x", "req")
    members = lax.axis_size(plane)
    requests = residual.shape[1]
    shape = jax.ShapeDtypeStruct

    rows, positions = key_cache.shape[1:3]
    partial, factor = call(
        attend_kernel,
        (shape((planes, 8, ROW), BF16), shape((requests // 2, LANES), F32)),
        [hbm()] * 8,
        [
            pltpu.VMEM(queries.shape, BF16),
            pltpu.VMEM((rows, positions, D), BF16),
            pltpu.VMEM((rows, positions, D), BF16),
            pltpu.VMEM(new_entries.shape, BF16),
            pltpu.SMEM(lengths.shape, jnp.int32),
            pltpu.SMEM(attention_ids.shape[::-1], jnp.int32),
            pltpu.SMEM(tenant_sizes.shape, jnp.int32),
            pltpu.SMEM(guidance.shape, jnp.int32),
            pltpu.VMEM((2, TOPK, 8, ROW), F32),
            pltpu.SemaphoreType.DMA((6,)),
            pltpu.SemaphoreType.DMA((rows,)),
            pltpu.SemaphoreType.DMA((rows,)),
        ],
    )(
        *(
            pltpu.with_memory_space_constraint(operand, pltpu.HBM)
            for operand in (
                queries,
                key_cache,
                value_cache,
                new_entries,
                lengths,
                attention_ids.T,
                tenant_sizes,
                guidance,
            )
        )
    )
    partial = exchanged(partial, "z")

    weight_rows = attention_output.shape[0]
    merged_rows = HEADS_ROW * 8 + 8 + weight_rows
    both, gains, ids = call(
        merge_kernel,
        (
            shape((members, merged_rows, LANES), BF16),
            shape((2, D), F32),
            shape((TOPK, requests), jnp.int32),
        ),
        [vmem()] * 5,
    )(partial, attention_output, expert_gain, final_gain, expert_ids.T)
    both = exchanged(both, plane)

    chunk = shape((planes, requests, LANES), BF16)
    projected = call(
        project_kernel,
        chunk,
        [vmem()] * 4,
        [pltpu.VMEM((members, 8, LANES), F32), pltpu.VMEM((members * weight_rows, LANES), BF16)],
    )(both, residual, attention_router.T, attention_ids.T)
    projected = exchanged(projected, "z")

    spread = shape((members, requests, LANES), BF16)
    attention = call(fold_kernel, spread, [vmem()])(projected)
    attention = exchanged(attention, plane)

    hidden = call(
        expert_kernel, spread, [vmem()] * 8, [pltpu.VMEM((requests, D), F32)]
    )(
        attention,
        residual,
        gains,
        expert_router.T,
        ids,
        expert_gate,
        expert_up,
        expert_down,
    )
    hidden = exchanged(hidden, plane)
    hidden = call(fold_kernel, chunk, [vmem()])(hidden)
    hidden = exchanged(hidden, "z")

    streams = lax.axis_size("cfg")
    final = call(
        finish_kernel, shape((streams * members, requests // 2, LANES), BF16), [vmem()] * 3
    )(hidden, projected, residual)
    final = exchanged(final, ("cfg",) + plane)

    return call(
        head_kernel,
        shape((requests // 2, unembedding.shape[0]), F32),
        [vmem()] * 4,
        [pltpu.VMEM((requests, D), F32)],
    )(final, gains, unembedding, factor)


def solution(mesh):
    sizes = mesh.devices.shape
    split = Mesh(mesh.devices.reshape(sizes[0], 16, sizes[1] // 16, sizes[2]), ("cfg", "z", "x", "req"))
    blk = ("z", "x")
    rows = P(("z", "x", "req"), None)
    placed = (
        P("cfg", None, None),
        P("cfg", "req", None),
        P("cfg", "req", None, None),
        P("cfg", "req", blk, None),
        P("cfg", "req", blk, None),
        P("cfg", "req"),
        P(),
        P(),
        P(),
        P(),
        rows,
        P(),
        rows,
        rows,
        rows,
        P(),
        rows,
        P(),
        P(),
    )
    return jax.shard_map(
        local,
        mesh=split,
        in_specs=placed,
        out_specs=P("cfg", ("z", "x", "req")),
        check_vma=False,
    )
```

```python
import math

import jax
import jax.numpy as jnp
from jax import lax
from jax.experimental import pallas as pl
from jax.experimental.pallas import tpu as pltpu
from jax.sharding import Mesh
from jax.sharding import PartitionSpec as P

D = 2048
H = 16
HD = 128
FF = 5632
TOPK = 2
EPS = 1e-05
NEG = -1e30
SPARE = 8
LANES = 128
HEADS_ROW = 4
ROW = HEADS_ROW * HD + LANES
SCALE = 1.0 / math.sqrt(HD)

F32 = jnp.float32
BF16 = jnp.bfloat16
NT = (((1,), (1,)), ((), ()))


def vmem():
    return pl.BlockSpec(memory_space=pltpu.VMEM)


def hbm():
    return pl.BlockSpec(memory_space=pltpu.HBM)


def call(body, outs, specs, scratch=()):
    return pl.pallas_call(
        body,
        out_shape=outs,
        in_specs=specs,
        out_specs=jax.tree.map(lambda _: vmem(), outs),
        scratch_shapes=list(scratch),
        compiler_params=pltpu.CompilerParams(vmem_limit_bytes=48 * 1024 * 1024),
    )


def iota(shape, dim):
    return lax.broadcasted_iota(jnp.int32, shape, dim)


def dot(a, b):
    return jnp.dot(a, b, preferred_element_type=F32)


def rms(values):
    return lax.rsqrt(jnp.mean(values * values, axis=-1, keepdims=True) + EPS)


def expert_of_plane():
    return lax.axis_index("z") // 2


def share_column(logits_t, ids_ref, expert, lane_of_row):
    experts = iota(logits_t.shape, 0)
    first_id, second_id = ids_ref[0:1, :], ids_ref[1:2, :]
    first = jnp.sum(jnp.where(experts == first_id, logits_t, 0.0), axis=0, keepdims=True)
    second = jnp.sum(jnp.where(experts == second_id, logits_t, 0.0), axis=0, keepdims=True)
    gate_first = 1.0 / (1.0 + jnp.exp(second - first))
    gate_second = 1.0 / (1.0 + jnp.exp(first - second))
    share = jnp.where(first_id == expert, gate_first, 0.0) + jnp.where(
        second_id == expert, gate_second, 0.0
    )
    lanes = iota((lane_of_row.shape[0], share.shape[1]), 1)
    return jnp.sum(jnp.where(lanes == lane_of_row, share, 0.0), axis=1, keepdims=True)


def guidance_factor(sizes_ref, guidance_ref, half):
    request = lax.axis_index("cfg") * half + iota((half, 1), 0)
    tenants = sizes_ref.shape[0]
    tenant = jnp.zeros((half, 1), jnp.int32)
    end = 0
    for t in range(tenants):
        end = end + sizes_ref[t]
        tenant = tenant + (request >= end).astype(jnp.int32)
    chosen = jnp.zeros((half, 1), jnp.int32)
    for t in range(tenants):
        chosen = jnp.where(tenant == t, guidance_ref[t], chosen)
    return chosen.astype(F32) / 4.0


def attend_kernel(
    q_hbm,
    k_hbm,
    v_hbm,
    new_hbm,
    lengths_hbm,
    ids_hbm,
    sizes_hbm,
    guidance_hbm,
    expert_ids_hbm,
    out_ref,
    factor_ref,
    expert_ids_ref,
    q_ref,
    k_ref,
    v_ref,
    new_ref,
    lengths_ref,
    ids_ref,
    sizes_ref,
    guidance_ref,
    rows_ref,
    small_sems,
    key_sems,
    value_sems,
):
    requests, positions = k_hbm.shape[1], k_hbm.shape[2]
    small = [
        pltpu.make_async_copy(source, target, small_sems.at[n])
        for n, (source, target) in enumerate(
            [
                (q_hbm, q_ref),
                (new_hbm, new_ref),
                (lengths_hbm, lengths_ref),
                (ids_hbm, ids_ref),
                (sizes_hbm, sizes_ref),
                (guidance_hbm, guidance_ref),
                (expert_ids_hbm, expert_ids_ref),
            ]
        )
    ]
    keys = [
        pltpu.make_async_copy(k_hbm.at[0, r], k_ref.at[r, :positions], key_sems.at[r])
        for r in range(requests)
    ]
    values_in = [
        pltpu.make_async_copy(v_hbm.at[0, r], v_ref.at[r, :positions], value_sems.at[r])
        for r in range(requests)
    ]
    for copy in small:
        copy.start()
    for key, value in zip(keys, values_in):
        key.start()
        value.start()
    block = lax.axis_index("z") * lax.axis_size("x") + lax.axis_index("x")
    owner = block == 0
    v_ref[:, positions:, :] = jnp.zeros((requests, SPARE, D), BF16)
    for copy in small:
        copy.wait()

    @pl.when(owner)
    def _():
        for r in range(requests):
            entry = new_ref[0, r].astype(F32)
            first = iota((SPARE, D), 0) == 0
            k_ref[r, positions:, :] = jnp.where(first, entry[0:1, :], 0.0).astype(BF16)
            v_ref[r, positions:, :] = jnp.where(first, entry[1:2, :], 0.0).astype(BF16)

    factor_ref[...] = jnp.broadcast_to(
        guidance_factor(sizes_ref, guidance_ref, factor_ref.shape[0]), factor_ref.shape
    )
    first_request = lax.axis_index("req") * requests
    queries = q_ref[0].astype(F32)
    own_head = iota((H, D), 0) == iota((H, D), 1) // HD
    column = iota((1, positions + SPARE), 1)
    place = block * positions + column
    cached = column < positions
    fresh = (column == positions) & owner
    sub = iota((8, LANES), 0)
    lane = iota((8, LANES), 1)
    for r in range(requests):
        wide = jnp.concatenate(
            [
                jnp.where(own_head, queries[r : r + 1, k * D : (k + 1) * D], 0.0)
                for k in range(TOPK)
            ],
            axis=0,
        )
        keys[r].wait()
        scores = (
            lax.dot_general(wide.astype(BF16), k_ref[r], NT, preferred_element_type=F32) * SCALE
        )
        live = (cached & (place < lengths_ref[0, r])) | fresh
        top = jnp.max(jnp.where(live, scores, NEG), axis=1, keepdims=True)
        peak = top.astype(BF16).astype(F32)
        weights = jnp.where(live, jnp.exp(scores - peak), 0.0)
        total = jnp.sum(weights, axis=1, keepdims=True)
        high = total.astype(BF16).astype(F32)
        low = total - high
        values_in[r].wait()
        values = dot(weights.astype(BF16), v_ref[r])
        for k in range(TOPK):
            for quarter in range(H // HEADS_ROW):
                half, group = quarter // 2, quarter % 2
                base = k * H + (quarter // 2) * 8
                parts = []
                for j in range(HEADS_ROW):
                    head = quarter * HEADS_ROW + j
                    tile = values[base : base + 8, head * HD : (head + 1) * HD]
                    parts.append(jnp.sum(jnp.where(sub == head % 8, tile, 0.0), axis=0, keepdims=True))
                part = sub - group * HEADS_ROW
                here = (part >= 0) & (part < HEADS_ROW)
                stats = jnp.where(lane == part, peak[base : base + 8], 0.0)
                stats = stats + jnp.where(lane == part + 4, high[base : base + 8], 0.0)
                stats = stats + jnp.where(lane == part + 8, low[base : base + 8], 0.0)
                parts.append(jnp.sum(jnp.where(here, stats, 0.0), axis=0, keepdims=True))
                row = group * requests + r
                rows_ref[half, k, row : row + 1, :] = jnp.concatenate(parts, axis=1)
    request = iota((8, 1), 0) % requests
    chosen = []
    for k in range(TOPK):
        picked = jnp.zeros((8, 1), jnp.int32)
        for r in range(requests):
            picked = jnp.where(request == r, ids_ref[k, first_request + r], picked)
        chosen.append(picked)
    for plane in range(out_ref.shape[0]):
        expert, half = plane // 2, plane % 2
        message = jnp.where(chosen[0] == expert, rows_ref[half, 0], 0.0)
        message = message + jnp.where(chosen[1] == expert, rows_ref[half, 1], 0.0)
        out_ref[plane] = message.astype(BF16)


def spread_lanes(first_lane):
    rows, columns = iota((LANES, HEADS_ROW * HD), 0), iota((LANES, HEADS_ROW * HD), 1)
    return rows == first_lane + columns // HD


def merged(parts, stats, groups):
    count = stats.shape[0]
    peak = jnp.max(stats, axis=0)
    scale = jnp.exp(stats - peak[None])
    rows = count * groups * 8
    flat = scale.reshape(rows, LANES)
    high = flat.astype(BF16)
    low = (flat - high.astype(F32)).astype(BF16)
    lift = spread_lanes(0).astype(BF16)
    scales = dot(high, lift) + dot(low, lift)
    sums = dot(
        stats.reshape(rows, LANES).astype(BF16), (spread_lanes(4) | spread_lanes(8)).astype(BF16)
    )
    numerator, denominator = [], []
    for g in range(groups):
        top, bottom = 0.0, 0.0
        for n in range(count):
            at = (n * groups + g) * 8
            factor = scales[at : at + 8]
            top = top + parts(n, g) * factor
            bottom = bottom + sums[at : at + 8] * factor
        numerator.append(top)
        denominator.append(bottom)
    return numerator, denominator, peak


def merge_kernel(
    in_ref, weight_ref, first_gain_ref, second_gain_ref, out_ref, gains_ref
):
    gains_ref[0, :] = first_gain_ref[...].astype(F32)
    gains_ref[1, :] = second_gain_ref[...].astype(F32)
    wide = HEADS_ROW * HD
    copies = out_ref.shape[0]
    stats = in_ref[:, :, wide:].astype(F32)[:, None]
    numerator, denominator, peak = merged(
        lambda n, g: in_ref[n, :, :wide].astype(F32), stats, 1
    )
    lane = iota((8, LANES), 1)
    packed = jnp.where(lane < HEADS_ROW, peak[0], 0.0)
    for j in range(HEADS_ROW):
        total = denominator[0][:, j * HD : (j + 1) * HD]
        high = total.astype(BF16).astype(F32)
        packed = jnp.where(lane == 4 + j, high, packed)
        packed = jnp.where(lane == 8 + j, total - high, packed)
    blocks = [numerator[0][:, j * HD : (j + 1) * HD] for j in range(HEADS_ROW)] + [packed]
    blocks = [block.astype(BF16) for block in blocks]
    for copy in range(copies):
        for j, block in enumerate(blocks):
            out_ref[copy, j * 8 : (j + 1) * 8, :] = block
        out_ref[copy, len(blocks) * 8 :, :] = weight_ref[:, copy * LANES : (copy + 1) * LANES]


def project_kernel(in_ref, residual_ref, router_ref, ids_ref, out_ref, stats_ref, weight_ref):
    requests = 4
    columns, groups = 4, 4
    head_rows = HEADS_ROW * 8
    weight_rows = in_ref.shape[1] - head_rows - 8
    sources = in_ref.shape[0]
    expert = expert_of_plane()
    for source in range(sources):
        stats_ref[source] = in_ref[source, head_rows : head_rows + 8, :].astype(F32)
        weight_ref[source * weight_rows : (source + 1) * weight_rows, :] = in_ref[
            source, head_rows + 8 :, :
        ]
    stats = stats_ref[...].reshape(columns, groups, 8, LANES)

    def part(n, g):
        source = n * groups + g
        return jnp.concatenate(
            [in_ref[source, j * 8 : (j + 1) * 8, :] for j in range(HEADS_ROW)], axis=1
        ).astype(F32)

    numerator, denominator, _ = merged(part, stats, groups)
    inputs = residual_ref[0].astype(F32)
    normed = (inputs * rms(inputs)).astype(BF16)
    logits = lax.dot_general(router_ref[...], normed, NT, preferred_element_type=F32)
    row = iota((8 * groups, 1), 0)
    gate = share_column(logits, ids_ref, expert, row // 8 * requests + row % requests)
    attended = jnp.concatenate(
        [top / jnp.maximum(bottom, 1e-30) for top, bottom in zip(numerator, denominator)], axis=0
    )
    gated = (attended.astype(BF16).astype(F32) * gate).astype(BF16)
    wide = HEADS_ROW * HD
    lower = dot(gated, weight_ref[:wide, :])
    upper = dot(gated, weight_ref[wide:, :])
    mixed = jnp.where(row % 8 < requests, lower, upper)
    sub = iota((8, LANES), 0)
    tiles = []
    for g in range(groups):
        tile = mixed[g * 8 : (g + 1) * 8]
        tiles.append(tile + pltpu.roll(tile, 4, 0))
    for pair in range(groups // 2):
        both = jnp.where(sub < requests, tiles[2 * pair], tiles[2 * pair + 1]).astype(BF16)
        for copy in range(out_ref.shape[0]):
            out_ref[copy, pair * 8 : (pair + 1) * 8, :] = both


def fold_kernel(in_ref, out_ref):
    total = in_ref[0].astype(F32)
    for n in range(1, in_ref.shape[0]):
        total = total + in_ref[n].astype(F32)
    total = total.astype(BF16)
    for copy in range(out_ref.shape[0]):
        out_ref[copy] = total


def expert_kernel(
    in_ref, residual_ref, gain_ref, router_ref, ids_ref, gate_ref, up_ref, down_ref, out_ref, middle_ref
):
    chunks = in_ref.shape[0]
    requests = in_ref.shape[1]
    for chunk in range(chunks):
        at = slice(chunk * LANES, (chunk + 1) * LANES)
        middle_ref[:, at] = residual_ref[0, :, at].astype(F32) + in_ref[chunk].astype(F32)
    middle = middle_ref[...]
    inputs = (middle * rms(middle) * gain_ref[0:1, :]).astype(BF16)
    logits = lax.dot_general(router_ref[...], inputs, NT, preferred_element_type=F32)
    share = share_column(logits, ids_ref, expert_of_plane(), iota((requests, 1), 0))
    gate = lax.dot_general(inputs, gate_ref[...], NT, preferred_element_type=F32)
    up = lax.dot_general(inputs, up_ref[...], NT, preferred_element_type=F32)
    hidden = (gate / (1.0 + jnp.exp(-gate)) * up * share).astype(BF16)
    for chunk in range(chunks):
        at = slice(chunk * LANES, (chunk + 1) * LANES)
        out_ref[chunk] = dot(hidden, down_ref[:, at]).astype(BF16)


def finish_kernel(in_ref, attention_ref, residual_ref, out_ref):
    total = attention_ref[0].astype(F32)
    for n in range(1, attention_ref.shape[0]):
        total = total + attention_ref[n].astype(F32)
    for n in range(in_ref.shape[0]):
        total = total + in_ref[n].astype(F32)
    chunk = lax.axis_index("x") * lax.axis_size("req") + lax.axis_index("req")
    at = pl.ds(pl.multiple_of(chunk * LANES, LANES), LANES)
    total = (total + residual_ref[0, :, at].astype(F32)).astype(out_ref.dtype)
    half = out_ref.shape[1]
    copies = out_ref.shape[0] // 2
    for stream in range(2):
        for copy in range(copies):
            out_ref[stream * copies + copy] = total[stream * half : (stream + 1) * half]


def head_kernel(in_ref, gain_ref, words_ref, factor_ref, out_ref, joined_ref):
    half = in_ref.shape[1]
    chunks = in_ref.shape[0] // 2
    for stream in range(2):
        for chunk in range(chunks):
            at = slice(chunk * LANES, (chunk + 1) * LANES)
            joined_ref[stream * half : (stream + 1) * half, at] = in_ref[
                stream * chunks + chunk
            ].astype(F32)
    joined = joined_ref[...]
    inputs = (joined * rms(joined) * gain_ref[1:2, :]).astype(BF16)
    logits = lax.dot_general(inputs, words_ref[...], NT, preferred_element_type=F32)
    factor = factor_ref[:, :1]
    conditional, unconditional = logits[:half], logits[half:]
    out_ref[...] = unconditional + factor * (conditional - unconditional)


def exchanged(value, axis):
    return lax.all_to_all(value, axis, 0, 0, tiled=True)


def local(
    residual,
    queries,
    new_entries,
    key_cache,
    value_cache,
    lengths,
    attention_ids,
    expert_ids,
    attention_router,
    expert_router,
    attention_output,
    expert_gain,
    expert_gate,
    expert_up,
    expert_down,
    final_gain,
    unembedding,
    tenant_sizes,
    guidance,
):
    planes = lax.axis_size("z")
    plane = ("x", "req")
    members = lax.axis_size(plane)
    requests = residual.shape[1]
    shape = jax.ShapeDtypeStruct

    rows, positions = key_cache.shape[1:3]
    partial, factor, ids = call(
        attend_kernel,
        (
            shape((planes, 8, ROW), BF16),
            shape((requests // 2, LANES), F32),
            shape(expert_ids.shape[::-1], jnp.int32),
        ),
        [hbm()] * 9,
        [
            pltpu.VMEM(queries.shape, BF16),
            pltpu.VMEM((rows, positions + SPARE, D), BF16),
            pltpu.VMEM((rows, positions + SPARE, D), BF16),
            pltpu.VMEM(new_entries.shape, BF16),
            pltpu.SMEM(lengths.shape, jnp.int32),
            pltpu.SMEM(attention_ids.shape[::-1], jnp.int32),
            pltpu.SMEM(tenant_sizes.shape, jnp.int32),
            pltpu.SMEM(guidance.shape, jnp.int32),
            pltpu.VMEM((2, TOPK, 8, ROW), F32),
            pltpu.SemaphoreType.DMA((7,)),
            pltpu.SemaphoreType.DMA((rows,)),
            pltpu.SemaphoreType.DMA((rows,)),
        ],
    )(
        *(
            pltpu.with_memory_space_constraint(operand, pltpu.HBM)
            for operand in (
                queries,
                key_cache,
                value_cache,
                new_entries,
                lengths,
                attention_ids.T,
                tenant_sizes,
                guidance,
                expert_ids.T,
            )
        )
    )
    partial = exchanged(partial, "z")

    weight_rows = attention_output.shape[0]
    merged_rows = HEADS_ROW * 8 + 8 + weight_rows
    both, gains = call(
        merge_kernel,
        (shape((members, merged_rows, LANES), BF16), shape((2, D), F32)),
        [vmem()] * 4,
    )(partial, attention_output, expert_gain, final_gain)
    both = exchanged(both, plane)

    chunk = shape((planes, requests, LANES), BF16)
    projected = call(
        project_kernel,
        chunk,
        [vmem()] * 4,
        [pltpu.VMEM((members, 8, LANES), F32), pltpu.VMEM((members * weight_rows, LANES), BF16)],
    )(both, residual, attention_router.T, attention_ids.T)
    projected = exchanged(projected, "z")

    spread = shape((members, requests, LANES), BF16)
    attention = call(fold_kernel, spread, [vmem()])(projected)
    attention = exchanged(attention, plane)

    hidden = call(
        expert_kernel, spread, [vmem()] * 8, [pltpu.VMEM((requests, D), F32)]
    )(
        attention,
        residual,
        gains,
        expert_router.T,
        ids,
        expert_gate,
        expert_up,
        expert_down,
    )
    hidden = exchanged(hidden, plane)
    hidden = call(fold_kernel, chunk, [vmem()])(hidden)
    hidden = exchanged(hidden, "z")

    streams = lax.axis_size("cfg")
    final = call(
        finish_kernel, shape((streams * members, requests // 2, LANES), BF16), [vmem()] * 3
    )(hidden, projected, residual)
    final = exchanged(final, ("cfg",) + plane)

    return call(
        head_kernel,
        shape((requests // 2, unembedding.shape[0]), F32),
        [vmem()] * 4,
        [pltpu.VMEM((requests, D), F32)],
    )(final, gains, unembedding, factor)


def solution(mesh):
    sizes = mesh.devices.shape
    split = Mesh(mesh.devices.reshape(sizes[0], 16, sizes[1] // 16, sizes[2]), ("cfg", "z", "x", "req"))
    blk = ("z", "x")
    rows = P(("z", "x", "req"), None)
    placed = (
        P("cfg", None, None),
        P("cfg", "req", None),
        P("cfg", "req", None, None),
        P("cfg", "req", blk, None),
        P("cfg", "req", blk, None),
        P("cfg", "req"),
        P(),
        P(),
        P(),
        P(),
        rows,
        P(),
        rows,
        rows,
        rows,
        P(),
        rows,
        P(),
        P(),
    )
    return jax.shard_map(
        local,
        mesh=split,
        in_specs=placed,
        out_specs=P("cfg", ("z", "x", "req")),
        check_vma=False,
    )
```

```python
import math

import jax
import jax.numpy as jnp
from jax import lax
from jax.experimental import pallas as pl
from jax.experimental.pallas import tpu as pltpu
from jax.sharding import Mesh
from jax.sharding import PartitionSpec as P

D = 2048
H = 16
HD = 128
FF = 5632
TOPK = 2
EPS = 1e-05
NEG = -1e30
SPARE = 16
LANES = 128
HEADS_ROW = 4
ROW = HEADS_ROW * HD + LANES
SCALE = 1.0 / math.sqrt(HD)

F32 = jnp.float32
BF16 = jnp.bfloat16
NT = (((1,), (1,)), ((), ()))


def vmem():
    return pl.BlockSpec(memory_space=pltpu.VMEM)


def hbm():
    return pl.BlockSpec(memory_space=pltpu.HBM)


def call(body, outs, specs, scratch=()):
    return pl.pallas_call(
        body,
        out_shape=outs,
        in_specs=specs,
        out_specs=jax.tree.map(lambda _: vmem(), outs),
        scratch_shapes=list(scratch),
        compiler_params=pltpu.CompilerParams(vmem_limit_bytes=48 * 1024 * 1024),
    )


def iota(shape, dim):
    return lax.broadcasted_iota(jnp.int32, shape, dim)


def dot(a, b):
    return jnp.dot(a, b, preferred_element_type=F32)


def rms(values):
    return lax.rsqrt(jnp.mean(values * values, axis=-1, keepdims=True) + EPS)


def expert_of_plane():
    return lax.axis_index("z") // 2


def share_column(logits_t, ids_ref, expert, lane_of_row):
    experts = iota(logits_t.shape, 0)
    first_id, second_id = ids_ref[0:1, :], ids_ref[1:2, :]
    first = jnp.sum(jnp.where(experts == first_id, logits_t, 0.0), axis=0, keepdims=True)
    second = jnp.sum(jnp.where(experts == second_id, logits_t, 0.0), axis=0, keepdims=True)
    gate_first = 1.0 / (1.0 + jnp.exp(second - first))
    gate_second = 1.0 / (1.0 + jnp.exp(first - second))
    share = jnp.where(first_id == expert, gate_first, 0.0) + jnp.where(
        second_id == expert, gate_second, 0.0
    )
    lanes = iota((lane_of_row.shape[0], share.shape[1]), 1)
    return jnp.sum(jnp.where(lanes == lane_of_row, share, 0.0), axis=1, keepdims=True)


def guidance_factor(sizes_ref, guidance_ref, half):
    request = lax.axis_index("cfg") * half + iota((half, 1), 0)
    tenants = sizes_ref.shape[0]
    tenant = jnp.zeros((half, 1), jnp.int32)
    end = 0
    for t in range(tenants):
        end = end + sizes_ref[t]
        tenant = tenant + (request >= end).astype(jnp.int32)
    chosen = jnp.zeros((half, 1), jnp.int32)
    for t in range(tenants):
        chosen = jnp.where(tenant == t, guidance_ref[t], chosen)
    return chosen.astype(F32) / 4.0


def attend_kernel(
    q_hbm,
    k_hbm,
    v_hbm,
    new_hbm,
    lengths_hbm,
    ids_hbm,
    sizes_hbm,
    guidance_hbm,
    expert_ids_hbm,
    out_ref,
    factor_ref,
    expert_ids_ref,
    q_ref,
    k_ref,
    v_ref,
    new_ref,
    lengths_ref,
    ids_ref,
    sizes_ref,
    guidance_ref,
    rows_ref,
    small_sems,
    key_sems,
    value_sems,
):
    requests, positions = k_hbm.shape[1], k_hbm.shape[2]
    small = [
        pltpu.make_async_copy(source, target, small_sems.at[n])
        for n, (source, target) in enumerate(
            [
                (q_hbm, q_ref),
                (new_hbm, new_ref),
                (lengths_hbm, lengths_ref),
                (ids_hbm, ids_ref),
                (sizes_hbm, sizes_ref),
                (guidance_hbm, guidance_ref),
                (expert_ids_hbm, expert_ids_ref),
            ]
        )
    ]
    keys = [
        pltpu.make_async_copy(k_hbm.at[0, r], k_ref.at[r, :positions], key_sems.at[r])
        for r in range(requests)
    ]
    values_in = [
        pltpu.make_async_copy(v_hbm.at[0, r], v_ref.at[r, :positions], value_sems.at[r])
        for r in range(requests)
    ]
    small[0].start()
    for key in keys:
        key.start()
    for copy in small[1:]:
        copy.start()
    for value in values_in:
        value.start()
    block = lax.axis_index("z") * lax.axis_size("x") + lax.axis_index("x")
    owner = block == 0
    first_request = lax.axis_index("req") * requests
    own_head = iota((H, D), 0) == iota((H, D), 1) // HD
    small[0].wait()
    queries = q_ref[0].astype(F32)
    wide = [
        jnp.concatenate(
            [
                jnp.where(own_head, queries[r : r + 1, k * D : (k + 1) * D], 0.0)
                for k in range(TOPK)
            ],
            axis=0,
        ).astype(BF16)
        for r in range(requests)
    ]
    for copy in small[1:]:
        copy.wait()
    new_row = (iota((SPARE, D), 0) == 0) & owner
    for r in range(requests):
        entry = new_ref[0, r].astype(F32)
        k_ref[r, positions:, :] = jnp.where(new_row, entry[0:1, :], 0.0).astype(BF16)
        v_ref[r, positions:, :] = jnp.where(new_row, entry[1:2, :], 0.0).astype(BF16)
    factor_ref[...] = jnp.broadcast_to(
        guidance_factor(sizes_ref, guidance_ref, factor_ref.shape[0]), factor_ref.shape
    )
    for key in keys:
        key.wait()
    scores = jnp.concatenate(
        [
            lax.dot_general(wide[r], k_ref[r], NT, preferred_element_type=F32)
            for r in range(requests)
        ],
        axis=0,
    )
    scores = scores * SCALE
    heads = TOPK * H
    request_of_row = iota((requests * heads, 1), 0) // heads
    length = jnp.zeros((requests * heads, 1), jnp.int32)
    for r in range(requests):
        length = jnp.where(request_of_row == r, lengths_ref[0, r], length)
    column = iota(scores.shape, 1)
    live = (column < positions) & (block * positions + column < length)
    live = live | ((column == positions) & owner)
    top = jnp.max(jnp.where(live, scores, NEG), axis=1, keepdims=True)
    peaks = top.astype(BF16).astype(F32)
    weights = jnp.where(live, jnp.exp(scores - peaks), 0.0)
    totals = jnp.sum(weights, axis=1, keepdims=True)
    highs = totals.astype(BF16).astype(F32)
    lows = totals - highs
    weights = weights.astype(BF16)
    for value in values_in:
        value.wait()
    products = [dot(weights[r * heads : (r + 1) * heads], v_ref[r]) for r in range(requests)]
    sub = iota((8, LANES), 0)
    lane = iota((8, LANES), 1)
    for r in range(requests):
        at = slice(r * heads, (r + 1) * heads)
        values, peak, high, low = products[r], peaks[at], highs[at], lows[at]
        for k in range(TOPK):
            for quarter in range(H // HEADS_ROW):
                half, group = quarter // 2, quarter % 2
                base = k * H + (quarter // 2) * 8
                parts = []
                for j in range(HEADS_ROW):
                    head = quarter * HEADS_ROW + j
                    tile = values[base : base + 8, head * HD : (head + 1) * HD]
                    parts.append(jnp.sum(jnp.where(sub == head % 8, tile, 0.0), axis=0, keepdims=True))
                part = sub - group * HEADS_ROW
                here = (part >= 0) & (part < HEADS_ROW)
                stats = jnp.where(lane == part, peak[base : base + 8], 0.0)
                stats = stats + jnp.where(lane == part + 4, high[base : base + 8], 0.0)
                stats = stats + jnp.where(lane == part + 8, low[base : base + 8], 0.0)
                parts.append(jnp.sum(jnp.where(here, stats, 0.0), axis=0, keepdims=True))
                row = group * requests + r
                rows_ref[half, k, row : row + 1, :] = jnp.concatenate(parts, axis=1)
    request = iota((8, 1), 0) % requests
    chosen = []
    for k in range(TOPK):
        picked = jnp.zeros((8, 1), jnp.int32)
        for r in range(requests):
            picked = jnp.where(request == r, ids_ref[k, first_request + r], picked)
        chosen.append(picked)
    for plane in range(out_ref.shape[0]):
        expert, half = plane // 2, plane % 2
        message = jnp.where(chosen[0] == expert, rows_ref[half, 0], 0.0)
        message = message + jnp.where(chosen[1] == expert, rows_ref[half, 1], 0.0)
        out_ref[plane] = message.astype(BF16)


def spread_lanes(first_lane):
    rows, columns = iota((LANES, HEADS_ROW * HD), 0), iota((LANES, HEADS_ROW * HD), 1)
    return rows == first_lane + columns // HD


def merged(parts, stats, groups):
    count = stats.shape[0]
    peak = jnp.max(stats, axis=0)
    scale = jnp.exp(stats - peak[None])
    rows = count * groups * 8
    flat = scale.reshape(rows, LANES)
    high = flat.astype(BF16)
    low = (flat - high.astype(F32)).astype(BF16)
    lift = spread_lanes(0).astype(BF16)
    scales = dot(high, lift) + dot(low, lift)
    sums = dot(
        stats.reshape(rows, LANES).astype(BF16), (spread_lanes(4) | spread_lanes(8)).astype(BF16)
    )
    numerator, denominator = [], []
    for g in range(groups):
        top, bottom = 0.0, 0.0
        for n in range(count):
            at = (n * groups + g) * 8
            factor = scales[at : at + 8]
            top = top + parts(n, g) * factor
            bottom = bottom + sums[at : at + 8] * factor
        numerator.append(top)
        denominator.append(bottom)
    return numerator, denominator, peak


def merge_kernel(
    in_ref, weight_ref, first_gain_ref, second_gain_ref, out_ref, gains_ref
):
    gains_ref[0, :] = first_gain_ref[...].astype(F32)
    gains_ref[1, :] = second_gain_ref[...].astype(F32)
    wide = HEADS_ROW * HD
    copies = out_ref.shape[0]
    stats = in_ref[:, :, wide:].astype(F32)[:, None]
    numerator, denominator, peak = merged(
        lambda n, g: in_ref[n, :, :wide].astype(F32), stats, 1
    )
    lane = iota((8, LANES), 1)
    packed = jnp.where(lane < HEADS_ROW, peak[0], 0.0)
    for j in range(HEADS_ROW):
        total = denominator[0][:, j * HD : (j + 1) * HD]
        high = total.astype(BF16).astype(F32)
        packed = jnp.where(lane == 4 + j, high, packed)
        packed = jnp.where(lane == 8 + j, total - high, packed)
    blocks = [numerator[0][:, j * HD : (j + 1) * HD] for j in range(HEADS_ROW)] + [packed]
    blocks = [block.astype(BF16) for block in blocks]
    for copy in range(copies):
        for j, block in enumerate(blocks):
            out_ref[copy, j * 8 : (j + 1) * 8, :] = block
        out_ref[copy, len(blocks) * 8 :, :] = weight_ref[:, copy * LANES : (copy + 1) * LANES]


def project_kernel(in_ref, residual_ref, router_ref, ids_ref, out_ref, stats_ref, weight_ref):
    requests = 4
    columns, groups = 4, 4
    head_rows = HEADS_ROW * 8
    weight_rows = in_ref.shape[1] - head_rows - 8
    sources = in_ref.shape[0]
    expert = expert_of_plane()
    for source in range(sources):
        stats_ref[source] = in_ref[source, head_rows : head_rows + 8, :].astype(F32)
        weight_ref[source * weight_rows : (source + 1) * weight_rows, :] = in_ref[
            source, head_rows + 8 :, :
        ]
    stats = stats_ref[...].reshape(columns, groups, 8, LANES)

    def part(n, g):
        source = n * groups + g
        return jnp.concatenate(
            [in_ref[source, j * 8 : (j + 1) * 8, :] for j in range(HEADS_ROW)], axis=1
        ).astype(F32)

    numerator, denominator, _ = merged(part, stats, groups)
    inputs = residual_ref[0].astype(F32)
    normed = (inputs * rms(inputs)).astype(BF16)
    logits = lax.dot_general(router_ref[...], normed, NT, preferred_element_type=F32)
    row = iota((8 * groups, 1), 0)
    gate = share_column(logits, ids_ref, expert, row // 8 * requests + row % requests)
    attended = jnp.concatenate(
        [top / jnp.maximum(bottom, 1e-30) for top, bottom in zip(numerator, denominator)], axis=0
    )
    gated = (attended.astype(BF16).astype(F32) * gate).astype(BF16)
    wide = HEADS_ROW * HD
    lower = dot(gated, weight_ref[:wide, :])
    upper = dot(gated, weight_ref[wide:, :])
    mixed = jnp.where(row % 8 < requests, lower, upper)
    sub = iota((8, LANES), 0)
    tiles = []
    for g in range(groups):
        tile = mixed[g * 8 : (g + 1) * 8]
        tiles.append(tile + pltpu.roll(tile, 4, 0))
    for pair in range(groups // 2):
        both = jnp.where(sub < requests, tiles[2 * pair], tiles[2 * pair + 1]).astype(BF16)
        for copy in range(out_ref.shape[0]):
            out_ref[copy, pair * 8 : (pair + 1) * 8, :] = both


def fold_kernel(in_ref, out_ref):
    total = in_ref[0].astype(F32)
    for n in range(1, in_ref.shape[0]):
        total = total + in_ref[n].astype(F32)
    total = total.astype(BF16)
    for copy in range(out_ref.shape[0]):
        out_ref[copy] = total


def expert_kernel(
    in_ref, residual_ref, gain_ref, router_ref, ids_ref, gate_ref, up_ref, down_ref, out_ref, middle_ref
):
    chunks = in_ref.shape[0]
    requests = in_ref.shape[1]
    for chunk in range(chunks):
        at = slice(chunk * LANES, (chunk + 1) * LANES)
        middle_ref[:, at] = residual_ref[0, :, at].astype(F32) + in_ref[chunk].astype(F32)
    middle = middle_ref[...]
    inputs = (middle * rms(middle) * gain_ref[0:1, :]).astype(BF16)
    logits = lax.dot_general(router_ref[...], inputs, NT, preferred_element_type=F32)
    share = share_column(logits, ids_ref, expert_of_plane(), iota((requests, 1), 0))
    gate = lax.dot_general(inputs, gate_ref[...], NT, preferred_element_type=F32)
    up = lax.dot_general(inputs, up_ref[...], NT, preferred_element_type=F32)
    hidden = (gate / (1.0 + jnp.exp(-gate)) * up * share).astype(BF16)
    for chunk in range(chunks):
        at = slice(chunk * LANES, (chunk + 1) * LANES)
        out_ref[chunk] = dot(hidden, down_ref[:, at]).astype(BF16)


def finish_kernel(in_ref, attention_ref, residual_ref, out_ref):
    total = attention_ref[0].astype(F32)
    for n in range(1, attention_ref.shape[0]):
        total = total + attention_ref[n].astype(F32)
    for n in range(in_ref.shape[0]):
        total = total + in_ref[n].astype(F32)
    chunk = lax.axis_index("x") * lax.axis_size("req") + lax.axis_index("req")
    at = pl.ds(pl.multiple_of(chunk * LANES, LANES), LANES)
    total = (total + residual_ref[0, :, at].astype(F32)).astype(out_ref.dtype)
    half = out_ref.shape[1]
    copies = out_ref.shape[0] // 2
    for stream in range(2):
        for copy in range(copies):
            out_ref[stream * copies + copy] = total[stream * half : (stream + 1) * half]


def head_kernel(in_ref, gain_ref, words_ref, factor_ref, out_ref, joined_ref):
    half = in_ref.shape[1]
    chunks = in_ref.shape[0] // 2
    for stream in range(2):
        for chunk in range(chunks):
            at = slice(chunk * LANES, (chunk + 1) * LANES)
            joined_ref[stream * half : (stream + 1) * half, at] = in_ref[
                stream * chunks + chunk
            ].astype(F32)
    joined = joined_ref[...]
    inputs = (joined * rms(joined) * gain_ref[1:2, :]).astype(BF16)
    logits = lax.dot_general(inputs, words_ref[...], NT, preferred_element_type=F32)
    factor = factor_ref[:, :1]
    conditional, unconditional = logits[:half], logits[half:]
    out_ref[...] = unconditional + factor * (conditional - unconditional)


def exchanged(value, axis):
    return lax.all_to_all(value, axis, 0, 0, tiled=True)


def local(
    residual,
    queries,
    new_entries,
    key_cache,
    value_cache,
    lengths,
    attention_ids,
    expert_ids,
    attention_router,
    expert_router,
    attention_output,
    expert_gain,
    expert_gate,
    expert_up,
    expert_down,
    final_gain,
    unembedding,
    tenant_sizes,
    guidance,
):
    planes = lax.axis_size("z")
    plane = ("x", "req")
    members = lax.axis_size(plane)
    requests = residual.shape[1]
    shape = jax.ShapeDtypeStruct

    rows, positions = key_cache.shape[1:3]
    partial, factor, ids = call(
        attend_kernel,
        (
            shape((planes, 8, ROW), BF16),
            shape((requests // 2, LANES), F32),
            shape(expert_ids.shape[::-1], jnp.int32),
        ),
        [hbm()] * 9,
        [
            pltpu.VMEM(queries.shape, BF16),
            pltpu.VMEM((rows, positions + SPARE, D), BF16),
            pltpu.VMEM((rows, positions + SPARE, D), BF16),
            pltpu.VMEM(new_entries.shape, BF16),
            pltpu.SMEM(lengths.shape, jnp.int32),
            pltpu.SMEM(attention_ids.shape[::-1], jnp.int32),
            pltpu.SMEM(tenant_sizes.shape, jnp.int32),
            pltpu.SMEM(guidance.shape, jnp.int32),
            pltpu.VMEM((2, TOPK, 8, ROW), F32),
            pltpu.SemaphoreType.DMA((7,)),
            pltpu.SemaphoreType.DMA((rows,)),
            pltpu.SemaphoreType.DMA((rows,)),
        ],
    )(
        *(
            pltpu.with_memory_space_constraint(operand, pltpu.HBM)
            for operand in (
                queries,
                key_cache,
                value_cache,
                new_entries,
                lengths,
                attention_ids.T,
                tenant_sizes,
                guidance,
                expert_ids.T,
            )
        )
    )
    partial = exchanged(partial, "z")

    weight_rows = attention_output.shape[0]
    merged_rows = HEADS_ROW * 8 + 8 + weight_rows
    both, gains = call(
        merge_kernel,
        (shape((members, merged_rows, LANES), BF16), shape((2, D), F32)),
        [vmem()] * 4,
    )(partial, attention_output, expert_gain, final_gain)
    both = exchanged(both, plane)

    chunk = shape((planes, requests, LANES), BF16)
    projected = call(
        project_kernel,
        chunk,
        [vmem()] * 4,
        [pltpu.VMEM((members, 8, LANES), F32), pltpu.VMEM((members * weight_rows, LANES), BF16)],
    )(both, residual, attention_router.T, attention_ids.T)
    projected = exchanged(projected, "z")

    spread = shape((members, requests, LANES), BF16)
    attention = call(fold_kernel, spread, [vmem()])(projected)
    attention = exchanged(attention, plane)

    hidden = call(
        expert_kernel, spread, [vmem()] * 8, [pltpu.VMEM((requests, D), F32)]
    )(
        attention,
        residual,
        gains,
        expert_router.T,
        ids,
        expert_gate,
        expert_up,
        expert_down,
    )
    hidden = exchanged(hidden, plane)
    hidden = call(fold_kernel, chunk, [vmem()])(hidden)
    hidden = exchanged(hidden, "z")

    streams = lax.axis_size("cfg")
    final = call(
        finish_kernel, shape((streams * members, requests // 2, LANES), BF16), [vmem()] * 3
    )(hidden, projected, residual)
    final = exchanged(final, ("cfg",) + plane)

    return call(
        head_kernel,
        shape((requests // 2, unembedding.shape[0]), F32),
        [vmem()] * 4,
        [pltpu.VMEM((requests, D), F32)],
    )(final, gains, unembedding, factor)


def solution(mesh):
    sizes = mesh.devices.shape
    split = Mesh(mesh.devices.reshape(sizes[0], 16, sizes[1] // 16, sizes[2]), ("cfg", "z", "x", "req"))
    blk = ("z", "x")
    rows = P(("z", "x", "req"), None)
    placed = (
        P("cfg", None, None),
        P("cfg", "req", None),
        P("cfg", "req", None, None),
        P("cfg", "req", blk, None),
        P("cfg", "req", blk, None),
        P("cfg", "req"),
        P(),
        P(),
        P(),
        P(),
        rows,
        P(),
        rows,
        rows,
        rows,
        P(),
        rows,
        P(),
        P(),
    )
    return jax.shard_map(
        local,
        mesh=split,
        in_specs=placed,
        out_specs=P("cfg", ("z", "x", "req")),
        check_vma=False,
    )
```

```python
import math

import jax
import jax.numpy as jnp
from jax import lax
from jax.experimental import pallas as pl
from jax.experimental.pallas import tpu as pltpu
from jax.sharding import Mesh
from jax.sharding import PartitionSpec as P

D = 2048
H = 16
HD = 128
FF = 5632
TOPK = 2
EPS = 1e-05
NEG = -1e30
SPARE = 16
LANES = 128
HEADS_ROW = 4
ROW = HEADS_ROW * HD + LANES
SCALE = 1.0 / math.sqrt(HD)

GATE_LANE = 12
GATE_TERMS = 3
MERGED = HEADS_ROW * 8 + 8

F32 = jnp.float32
BF16 = jnp.bfloat16
NT = (((1,), (1,)), ((), ()))


def vmem():
    return pl.BlockSpec(memory_space=pltpu.VMEM)


def hbm():
    return pl.BlockSpec(memory_space=pltpu.HBM)


def call(body, outs, specs, scratch=()):
    return pl.pallas_call(
        body,
        out_shape=outs,
        in_specs=specs,
        out_specs=jax.tree.map(lambda _: vmem(), outs),
        scratch_shapes=list(scratch),
        compiler_params=pltpu.CompilerParams(vmem_limit_bytes=48 * 1024 * 1024),
    )


def iota(shape, dim):
    return lax.broadcasted_iota(jnp.int32, shape, dim)


def dot(a, b):
    return jnp.dot(a, b, preferred_element_type=F32)


def rms(values):
    return lax.rsqrt(jnp.mean(values * values, axis=-1, keepdims=True) + EPS)


def expert_of_plane():
    return lax.axis_index("z") // 2


def share_column(logits_t, ids_ref, expert, lane_of_row):
    experts = iota(logits_t.shape, 0)
    first_id, second_id = ids_ref[0:1, :], ids_ref[1:2, :]
    first = jnp.sum(jnp.where(experts == first_id, logits_t, 0.0), axis=0, keepdims=True)
    second = jnp.sum(jnp.where(experts == second_id, logits_t, 0.0), axis=0, keepdims=True)
    gate_first = 1.0 / (1.0 + jnp.exp(second - first))
    gate_second = 1.0 / (1.0 + jnp.exp(first - second))
    share = jnp.where(first_id == expert, gate_first, 0.0) + jnp.where(
        second_id == expert, gate_second, 0.0
    )
    lanes = iota((lane_of_row.shape[0], share.shape[1]), 1)
    return jnp.sum(jnp.where(lanes == lane_of_row, share, 0.0), axis=1, keepdims=True)


def guidance_factor(sizes_ref, guidance_ref, half):
    request = lax.axis_index("cfg") * half + iota((half, 1), 0)
    tenants = sizes_ref.shape[0]
    tenant = jnp.zeros((half, 1), jnp.int32)
    end = 0
    for t in range(tenants):
        end = end + sizes_ref[t]
        tenant = tenant + (request >= end).astype(jnp.int32)
    chosen = jnp.zeros((half, 1), jnp.int32)
    for t in range(tenants):
        chosen = jnp.where(tenant == t, guidance_ref[t], chosen)
    return chosen.astype(F32) / 4.0


def attend_kernel(
    q_hbm,
    k_hbm,
    v_hbm,
    new_hbm,
    lengths_hbm,
    ids_hbm,
    sizes_hbm,
    guidance_hbm,
    expert_ids_hbm,
    out_ref,
    factor_ref,
    expert_ids_ref,
    q_ref,
    k_ref,
    v_ref,
    new_ref,
    lengths_ref,
    ids_ref,
    sizes_ref,
    guidance_ref,
    rows_ref,
    small_sems,
    key_sems,
    value_sems,
):
    requests, positions = k_hbm.shape[1], k_hbm.shape[2]
    small = [
        pltpu.make_async_copy(source, target, small_sems.at[n])
        for n, (source, target) in enumerate(
            [
                (q_hbm, q_ref),
                (new_hbm, new_ref),
                (lengths_hbm, lengths_ref),
                (ids_hbm, ids_ref),
                (sizes_hbm, sizes_ref),
                (guidance_hbm, guidance_ref),
                (expert_ids_hbm, expert_ids_ref),
            ]
        )
    ]
    keys = [
        pltpu.make_async_copy(k_hbm.at[0, r], k_ref.at[r, :positions], key_sems.at[r])
        for r in range(requests)
    ]
    values_in = [
        pltpu.make_async_copy(v_hbm.at[0, r], v_ref.at[r, :positions], value_sems.at[r])
        for r in range(requests)
    ]
    small[0].start()
    for key in keys:
        key.start()
    for copy in small[1:]:
        copy.start()
    for value in values_in:
        value.start()
    block = lax.axis_index("z") * lax.axis_size("x") + lax.axis_index("x")
    owner = block == 0
    first_request = lax.axis_index("req") * requests
    own_head = iota((H, D), 0) == iota((H, D), 1) // HD
    small[0].wait()
    queries = q_ref[0].astype(F32)
    wide = [
        jnp.concatenate(
            [
                jnp.where(own_head, queries[r : r + 1, k * D : (k + 1) * D], 0.0)
                for k in range(TOPK)
            ],
            axis=0,
        ).astype(BF16)
        for r in range(requests)
    ]
    for copy in small[1:]:
        copy.wait()
    new_row = (iota((SPARE, D), 0) == 0) & owner
    for r in range(requests):
        entry = new_ref[0, r].astype(F32)
        k_ref[r, positions:, :] = jnp.where(new_row, entry[0:1, :], 0.0).astype(BF16)
        v_ref[r, positions:, :] = jnp.where(new_row, entry[1:2, :], 0.0).astype(BF16)
    factor_ref[...] = jnp.broadcast_to(
        guidance_factor(sizes_ref, guidance_ref, factor_ref.shape[0]), factor_ref.shape
    )
    for key in keys:
        key.wait()
    scores = jnp.concatenate(
        [
            lax.dot_general(wide[r], k_ref[r], NT, preferred_element_type=F32)
            for r in range(requests)
        ],
        axis=0,
    )
    scores = scores * SCALE
    heads = TOPK * H
    request_of_row = iota((requests * heads, 1), 0) // heads
    length = jnp.zeros((requests * heads, 1), jnp.int32)
    for r in range(requests):
        length = jnp.where(request_of_row == r, lengths_ref[0, r], length)
    column = iota(scores.shape, 1)
    live = (column < positions) & (block * positions + column < length)
    live = live | ((column == positions) & owner)
    top = jnp.max(jnp.where(live, scores, NEG), axis=1, keepdims=True)
    peaks = top.astype(BF16).astype(F32)
    weights = jnp.where(live, jnp.exp(scores - peaks), 0.0)
    totals = jnp.sum(weights, axis=1, keepdims=True)
    highs = totals.astype(BF16).astype(F32)
    lows = totals - highs
    weights = weights.astype(BF16)
    for value in values_in:
        value.wait()
    products = [dot(weights[r * heads : (r + 1) * heads], v_ref[r]) for r in range(requests)]
    sub = iota((8, LANES), 0)
    lane = iota((8, LANES), 1)
    for r in range(requests):
        at = slice(r * heads, (r + 1) * heads)
        values, peak, high, low = products[r], peaks[at], highs[at], lows[at]
        for k in range(TOPK):
            for quarter in range(H // HEADS_ROW):
                half, group = quarter // 2, quarter % 2
                base = k * H + (quarter // 2) * 8
                parts = []
                for j in range(HEADS_ROW):
                    head = quarter * HEADS_ROW + j
                    tile = values[base : base + 8, head * HD : (head + 1) * HD]
                    parts.append(jnp.sum(jnp.where(sub == head % 8, tile, 0.0), axis=0, keepdims=True))
                part = sub - group * HEADS_ROW
                here = (part >= 0) & (part < HEADS_ROW)
                stats = jnp.where(lane == part, peak[base : base + 8], 0.0)
                stats = stats + jnp.where(lane == part + 4, high[base : base + 8], 0.0)
                stats = stats + jnp.where(lane == part + 8, low[base : base + 8], 0.0)
                parts.append(jnp.sum(jnp.where(here, stats, 0.0), axis=0, keepdims=True))
                row = group * requests + r
                rows_ref[half, k, row : row + 1, :] = jnp.concatenate(parts, axis=1)
    request = iota((8, 1), 0) % requests
    chosen = []
    for k in range(TOPK):
        picked = jnp.zeros((8, 1), jnp.int32)
        for r in range(requests):
            picked = jnp.where(request == r, ids_ref[k, first_request + r], picked)
        chosen.append(picked)
    for plane in range(out_ref.shape[0]):
        expert, half = plane // 2, plane % 2
        message = jnp.where(chosen[0] == expert, rows_ref[half, 0], 0.0)
        message = message + jnp.where(chosen[1] == expert, rows_ref[half, 1], 0.0)
        out_ref[plane] = message.astype(BF16)


def spread_lanes(first_lane):
    rows, columns = iota((LANES, HEADS_ROW * HD), 0), iota((LANES, HEADS_ROW * HD), 1)
    return rows == first_lane + columns // HD


def merged(parts, stats, groups):
    count = stats.shape[0]
    peak = jnp.max(stats, axis=0)
    scale = jnp.exp(stats - peak[None])
    rows = count * groups * 8
    flat = scale.reshape(rows, LANES)
    high = flat.astype(BF16)
    low = (flat - high.astype(F32)).astype(BF16)
    lift = spread_lanes(0).astype(BF16)
    scales = dot(high, lift) + dot(low, lift)
    sums = dot(
        stats.reshape(rows, LANES).astype(BF16), (spread_lanes(4) | spread_lanes(8)).astype(BF16)
    )
    numerator, denominator = [], []
    for g in range(groups):
        top, bottom = 0.0, 0.0
        for n in range(count):
            at = (n * groups + g) * 8
            factor = scales[at : at + 8]
            top = top + parts(n, g) * factor
            bottom = bottom + sums[at : at + 8] * factor
        numerator.append(top)
        denominator.append(bottom)
    return numerator, denominator, peak


def merge_kernel(
    in_ref, residual_ref, router_ref, ids_ref, first_gain_ref, second_gain_ref, out_ref, gains_ref
):
    gains_ref[0, :] = first_gain_ref[...].astype(F32)
    gains_ref[1, :] = second_gain_ref[...].astype(F32)
    wide = HEADS_ROW * HD
    stats = in_ref[:, :, wide:].astype(F32)[:, None]
    numerator, denominator, peak = merged(
        lambda n, g: in_ref[n, :, :wide].astype(F32), stats, 1
    )
    lane = iota((8, LANES), 1)
    packed = jnp.where(lane < HEADS_ROW, peak[0], 0.0)
    for j in range(HEADS_ROW):
        total = denominator[0][:, j * HD : (j + 1) * HD]
        high = total.astype(BF16).astype(F32)
        packed = jnp.where(lane == 4 + j, high, packed)
        packed = jnp.where(lane == 8 + j, total - high, packed)
    inputs = residual_ref[0].astype(F32)
    normed = (inputs * rms(inputs)).astype(BF16)
    logits = lax.dot_general(router_ref[...], normed, NT, preferred_element_type=F32)
    request = lax.axis_index("req") * 4 + iota((8, 1), 0) % 4
    rest = share_column(logits, ids_ref, expert_of_plane(), request)
    for term in range(GATE_TERMS):
        piece = rest.astype(BF16).astype(F32)
        packed = jnp.where(lane == GATE_LANE + term, piece, packed)
        rest = rest - piece
    chunk = lax.axis_index("x") * lax.axis_size("req") + lax.axis_index("req")
    features = pl.ds(pl.multiple_of(chunk * LANES, LANES), LANES)
    blocks = [numerator[0][:, j * HD : (j + 1) * HD] for j in range(HEADS_ROW)] + [packed]
    stream = lax.axis_index("cfg")
    for s in range(out_ref.shape[0]):
        for j, block in enumerate(blocks):
            at = slice(j * 8, (j + 1) * 8)
            out_ref[s, at, :] = jnp.where(stream == s, block, 0.0).astype(BF16)
        own = residual_ref[0, :, features].astype(F32)
        out_ref[s, len(blocks) * 8 :, :] = jnp.where(stream == s, own, 0.0).astype(BF16)


def pack_kernel(in_ref, weight_ref, out_ref):
    streams = in_ref.shape[0]
    for copy in range(out_ref.shape[0]):
        for s in range(streams):
            out_ref[copy, s * MERGED : (s + 1) * MERGED, :] = in_ref[s, :MERGED, :]
        out_ref[copy, streams * MERGED :, :] = weight_ref[:, copy * LANES : (copy + 1) * LANES]


def project_kernel(in_ref, out_ref, stats_ref, weight_ref):
    requests = 4
    columns, groups = 4, 4
    streams = stats_ref.shape[0]
    head_rows = HEADS_ROW * 8
    weight_at = streams * MERGED
    weight_rows = in_ref.shape[1] - weight_at
    sources = in_ref.shape[0]
    for source in range(sources):
        for s in range(streams):
            at = s * MERGED + head_rows
            stats_ref[s, source] = in_ref[source, at : at + 8, :].astype(F32)
        weight_ref[source * weight_rows : (source + 1) * weight_rows, :] = in_ref[
            source, weight_at:, :
        ]
    gated = []
    for s in range(streams):
        stats = stats_ref[s].reshape(columns, groups, 8, LANES)

        def part(n, g, base=s * MERGED):
            source = n * groups + g
            return jnp.concatenate(
                [in_ref[source, base + j * 8 : base + (j + 1) * 8, :] for j in range(HEADS_ROW)],
                axis=1,
            ).astype(F32)

        numerator, denominator, _ = merged(part, stats, groups)
        terms = stats_ref[s, :groups].reshape(8 * groups, LANES)
        lane = iota(terms.shape, 1)
        is_gate = (lane >= GATE_LANE) & (lane < GATE_LANE + GATE_TERMS)
        gate = jnp.sum(jnp.where(is_gate, terms, 0.0), axis=1, keepdims=True)
        attended = jnp.concatenate(
            [top / jnp.maximum(bottom, 1e-30) for top, bottom in zip(numerator, denominator)],
            axis=0,
        )
        gated.append((attended.astype(BF16).astype(F32) * gate).astype(BF16))
    gated = jnp.concatenate(gated, axis=0)
    wide = HEADS_ROW * HD
    lower = dot(gated, weight_ref[:wide, :])
    upper = dot(gated, weight_ref[wide:, :])
    mixed = jnp.where(iota((8 * groups * streams, 1), 0) % 8 < requests, lower, upper)
    sub = iota((8, LANES), 0)
    tiles = []
    for g in range(groups * streams):
        tile = mixed[g * 8 : (g + 1) * 8]
        tiles.append(tile + pltpu.roll(tile, 4, 0))
    for pair in range(groups * streams // 2):
        both = jnp.where(sub < requests, tiles[2 * pair], tiles[2 * pair + 1]).astype(BF16)
        for copy in range(out_ref.shape[0]):
            out_ref[copy, pair * 8 : (pair + 1) * 8, :] = both


def fold_kernel(in_ref, out_ref):
    total = in_ref[0].astype(F32)
    for n in range(1, in_ref.shape[0]):
        total = total + in_ref[n].astype(F32)
    total = total.astype(BF16)
    for copy in range(out_ref.shape[0]):
        out_ref[copy] = total


def middle_kernel(in_ref, own_ref, out_ref):
    total = in_ref[0].astype(F32)
    for n in range(1, in_ref.shape[0]):
        total = total + in_ref[n].astype(F32)
    requests = total.shape[0] // own_ref.shape[0]
    for s in range(own_ref.shape[0]):
        rows = slice(s * requests, (s + 1) * requests)
        middle = (total[rows] + own_ref[s, MERGED:, :].astype(F32)).astype(BF16)
        for copy in range(out_ref.shape[0]):
            out_ref[copy, rows, :] = middle


def expert_kernel(
    in_ref, gain_ref, router_ref, ids_ref, gate_ref, up_ref, down_ref, out_ref, middle_ref
):
    chunks = in_ref.shape[0]
    requests = ids_ref.shape[1]
    streams = in_ref.shape[1] // requests
    for chunk in range(chunks):
        at = slice(chunk * LANES, (chunk + 1) * LANES)
        middle_ref[:, at] = in_ref[chunk].astype(F32)
    middle = middle_ref[...]
    inputs = (middle * rms(middle) * gain_ref[0:1, :]).astype(BF16)
    shares = []
    for s in range(streams):
        rows = slice(s * requests, (s + 1) * requests)
        logits = lax.dot_general(router_ref[...], inputs[rows], NT, preferred_element_type=F32)
        shares.append(
            share_column(logits, ids_ref, expert_of_plane(), iota((requests, 1), 0))
        )
    share = jnp.concatenate(shares, axis=0)
    gate = lax.dot_general(inputs, gate_ref[...], NT, preferred_element_type=F32)
    up = lax.dot_general(inputs, up_ref[...], NT, preferred_element_type=F32)
    hidden = (gate / (1.0 + jnp.exp(-gate)) * up * share).astype(BF16)
    for chunk in range(chunks):
        at = slice(chunk * LANES, (chunk + 1) * LANES)
        out_ref[chunk] = dot(hidden, down_ref[:, at]).astype(BF16)


def finish_kernel(in_ref, attention_ref, own_ref, out_ref):
    total = attention_ref[0].astype(F32)
    for n in range(1, attention_ref.shape[0]):
        total = total + attention_ref[n].astype(F32)
    for n in range(in_ref.shape[0]):
        total = total + in_ref[n].astype(F32)
    streams = own_ref.shape[0]
    requests = total.shape[0] // streams
    half = requests // 2
    copies = out_ref.shape[0] // 2
    for s in range(streams):
        rows = total[s * requests : (s + 1) * requests] + own_ref[s, MERGED:, :].astype(F32)
        rows = rows.astype(out_ref.dtype)
        for core in range(2):
            for copy in range(copies):
                out_ref[core * copies + copy, s * half : (s + 1) * half, :] = rows[
                    core * half : (core + 1) * half
                ]


def head_kernel(in_ref, gain_ref, words_ref, factor_ref, out_ref, joined_ref):
    chunks = in_ref.shape[0] // 2
    half = out_ref.shape[0]
    for chunk in range(chunks):
        at = slice(chunk * LANES, (chunk + 1) * LANES)
        joined_ref[:, at] = in_ref[chunks + chunk].astype(F32)
    joined = joined_ref[...]
    inputs = (joined * rms(joined) * gain_ref[1:2, :]).astype(BF16)
    logits = lax.dot_general(inputs, words_ref[...], NT, preferred_element_type=F32)
    factor = factor_ref[:, :1]
    conditional, unconditional = logits[:half], logits[half:]
    out_ref[...] = unconditional + factor * (conditional - unconditional)


def exchanged(value, axis):
    return lax.all_to_all(value, axis, 0, 0, tiled=True)


def local(
    residual,
    queries,
    new_entries,
    key_cache,
    value_cache,
    lengths,
    attention_ids,
    expert_ids,
    attention_router,
    expert_router,
    attention_output,
    expert_gain,
    expert_gate,
    expert_up,
    expert_down,
    final_gain,
    unembedding,
    tenant_sizes,
    guidance,
):
    planes, streams = lax.axis_size("z"), lax.axis_size("cfg")
    plane = ("x", "req")
    members = lax.axis_size(plane)
    requests = residual.shape[1]
    shape = jax.ShapeDtypeStruct

    rows, positions = key_cache.shape[1:3]
    partial, factor, ids = call(
        attend_kernel,
        (
            shape((planes, 8, ROW), BF16),
            shape((requests // 2, LANES), F32),
            shape(expert_ids.shape[::-1], jnp.int32),
        ),
        [hbm()] * 9,
        [
            pltpu.VMEM(queries.shape, BF16),
            pltpu.VMEM((rows, positions + SPARE, D), BF16),
            pltpu.VMEM((rows, positions + SPARE, D), BF16),
            pltpu.VMEM(new_entries.shape, BF16),
            pltpu.SMEM(lengths.shape, jnp.int32),
            pltpu.SMEM(attention_ids.shape[::-1], jnp.int32),
            pltpu.SMEM(tenant_sizes.shape, jnp.int32),
            pltpu.SMEM(guidance.shape, jnp.int32),
            pltpu.VMEM((2, TOPK, 8, ROW), F32),
            pltpu.SemaphoreType.DMA((7,)),
            pltpu.SemaphoreType.DMA((rows,)),
            pltpu.SemaphoreType.DMA((rows,)),
        ],
    )(
        *(
            pltpu.with_memory_space_constraint(operand, pltpu.HBM)
            for operand in (
                queries,
                key_cache,
                value_cache,
                new_entries,
                lengths,
                attention_ids.T,
                tenant_sizes,
                guidance,
                expert_ids.T,
            )
        )
    )
    partial = exchanged(partial, "z")
    own, gains = call(
        merge_kernel,
        (shape((streams, MERGED + requests, LANES), BF16), shape((2, D), F32)),
        [vmem()] * 6,
    )(partial, residual, attention_router.T, attention_ids.T, expert_gain, final_gain)
    own = lax.psum(own, "cfg")

    def middle(own):
        weight_rows = attention_output.shape[0]
        packed = call(
            pack_kernel,
            shape((members, streams * MERGED + weight_rows, LANES), BF16),
            [vmem()] * 2,
        )(own, attention_output)
        packed = exchanged(packed, plane)

        chunk = shape((planes, streams * requests, LANES), BF16)
        projected = call(
            project_kernel,
            chunk,
            [vmem()],
            [
                pltpu.VMEM((streams, members, 8, LANES), F32),
                pltpu.VMEM((members * weight_rows, LANES), BF16),
            ],
        )(packed)
        projected = exchanged(projected, "z")

        spread = shape((members, streams * requests, LANES), BF16)
        attention = call(middle_kernel, spread, [vmem()] * 2)(projected, own)
        attention = exchanged(attention, plane)
        hidden = call(
            expert_kernel, spread, [vmem()] * 7, [pltpu.VMEM((streams * requests, D), F32)]
        )(attention, gains, expert_router.T, ids, expert_gate, expert_up, expert_down)
        hidden = exchanged(hidden, plane)
        hidden = call(fold_kernel, chunk, [vmem()])(hidden)
        hidden = exchanged(hidden, "z")
        return call(
            finish_kernel, shape((2 * members, requests, LANES), BF16), [vmem()] * 3
        )(hidden, projected, own)

    final = lax.cond(
        lax.axis_index("cfg") == 1,
        middle,
        lambda own: jnp.zeros((2 * members, requests, LANES), BF16),
        own,
    )
    final = exchanged(final, ("cfg",) + plane)
    return call(
        head_kernel,
        shape((requests // 2, unembedding.shape[0]), F32),
        [vmem()] * 4,
        [pltpu.VMEM((requests, D), F32)],
    )(final, gains, unembedding, factor)


def solution(mesh):
    sizes = mesh.devices.shape
    split = Mesh(mesh.devices.reshape(sizes[0], 16, sizes[1] // 16, sizes[2]), ("cfg", "z", "x", "req"))
    blk = ("z", "x")
    rows = P(("z", "x", "req"), None)
    placed = (
        P("cfg", None, None),
        P("cfg", "req", None),
        P("cfg", "req", None, None),
        P("cfg", "req", blk, None),
        P("cfg", "req", blk, None),
        P("cfg", "req"),
        P(),
        P(),
        P(),
        P(),
        rows,
        P(),
        rows,
        rows,
        rows,
        P(),
        rows,
        P(),
        P(),
    )
    return jax.shard_map(
        local,
        mesh=split,
        in_specs=placed,
        out_specs=P("cfg", ("z", "x", "req")),
        check_vma=False,
    )
```

```python
import math

import jax
import jax.numpy as jnp
from jax import lax
from jax.experimental import pallas as pl
from jax.experimental.pallas import tpu as pltpu
from jax.sharding import Mesh
from jax.sharding import PartitionSpec as P

D = 2048
H = 16
HD = 128
FF = 5632
TOPK = 2
EPS = 1e-05
NEG = -1e30
SPARE = 16
LANES = 128
HEADS_ROW = 4
ROW = HEADS_ROW * HD + LANES
SCALE = 1.0 / math.sqrt(HD)

F32 = jnp.float32
BF16 = jnp.bfloat16
NT = (((1,), (1,)), ((), ()))


def vmem():
    return pl.BlockSpec(memory_space=pltpu.VMEM)


def hbm():
    return pl.BlockSpec(memory_space=pltpu.HBM)


def call(body, outs, specs, scratch=()):
    return pl.pallas_call(
        body,
        out_shape=outs,
        in_specs=specs,
        out_specs=jax.tree.map(lambda _: vmem(), outs),
        scratch_shapes=list(scratch),
        compiler_params=pltpu.CompilerParams(vmem_limit_bytes=48 * 1024 * 1024),
    )


def iota(shape, dim):
    return lax.broadcasted_iota(jnp.int32, shape, dim)


def dot(a, b):
    return jnp.dot(a, b, preferred_element_type=F32)


def rms(values):
    return lax.rsqrt(jnp.mean(values * values, axis=-1, keepdims=True) + EPS)


def expert_of_plane():
    return lax.axis_index("z") // 2


def share_column(logits_t, ids_ref, expert, lane_of_row):
    experts = iota(logits_t.shape, 0)
    first_id, second_id = ids_ref[0:1, :], ids_ref[1:2, :]
    first = jnp.sum(jnp.where(experts == first_id, logits_t, 0.0), axis=0, keepdims=True)
    second = jnp.sum(jnp.where(experts == second_id, logits_t, 0.0), axis=0, keepdims=True)
    gate_first = 1.0 / (1.0 + jnp.exp(second - first))
    gate_second = 1.0 / (1.0 + jnp.exp(first - second))
    share = jnp.where(first_id == expert, gate_first, 0.0) + jnp.where(
        second_id == expert, gate_second, 0.0
    )
    lanes = iota((lane_of_row.shape[0], share.shape[1]), 1)
    return jnp.sum(jnp.where(lanes == lane_of_row, share, 0.0), axis=1, keepdims=True)


def guidance_factor(sizes_ref, guidance_ref, half):
    request = lax.axis_index("cfg") * half + iota((half, 1), 0)
    tenants = sizes_ref.shape[0]
    tenant = jnp.zeros((half, 1), jnp.int32)
    end = 0
    for t in range(tenants):
        end = end + sizes_ref[t]
        tenant = tenant + (request >= end).astype(jnp.int32)
    chosen = jnp.zeros((half, 1), jnp.int32)
    for t in range(tenants):
        chosen = jnp.where(tenant == t, guidance_ref[t], chosen)
    return chosen.astype(F32) / 4.0


def attend_kernel(
    q_hbm,
    k_hbm,
    v_hbm,
    new_hbm,
    lengths_hbm,
    ids_hbm,
    sizes_hbm,
    guidance_hbm,
    expert_ids_hbm,
    out_ref,
    factor_ref,
    expert_ids_ref,
    q_ref,
    k_ref,
    v_ref,
    new_ref,
    lengths_ref,
    ids_ref,
    sizes_ref,
    guidance_ref,
    rows_ref,
    small_sems,
    cache_sems,
):
    requests, positions = k_hbm.shape[1], k_hbm.shape[2]
    small = [
        pltpu.make_async_copy(source, target, small_sems.at[n])
        for n, (source, target) in enumerate(
            [
                (q_hbm, q_ref),
                (new_hbm, new_ref),
                (lengths_hbm, lengths_ref),
                (ids_hbm, ids_ref),
                (sizes_hbm, sizes_ref),
                (guidance_hbm, guidance_ref),
                (expert_ids_hbm, expert_ids_ref),
            ]
        )
    ]
    keys = pltpu.make_async_copy(k_hbm.at[0], k_ref.at[:, :positions], cache_sems.at[0])
    values_in = pltpu.make_async_copy(v_hbm.at[0], v_ref.at[:, :positions], cache_sems.at[1])
    keys.start()
    values_in.start()
    for copy in small:
        copy.start()
    block = lax.axis_index("z") * lax.axis_size("x") + lax.axis_index("x")
    owner = block == 0
    first_request = lax.axis_index("req") * requests
    own_head = iota((H, D), 0) == iota((H, D), 1) // HD
    for copy in [*small, keys, values_in]:
        copy.wait()
    queries = q_ref[0].astype(F32)
    wide = [
        jnp.concatenate(
            [
                jnp.where(own_head, queries[r : r + 1, k * D : (k + 1) * D], 0.0)
                for k in range(TOPK)
            ],
            axis=0,
        ).astype(BF16)
        for r in range(requests)
    ]
    new_row = (iota((SPARE, D), 0) == 0) & owner
    for r in range(requests):
        entry = new_ref[0, r].astype(F32)
        k_ref[r, positions:, :] = jnp.where(new_row, entry[0:1, :], 0.0).astype(BF16)
        v_ref[r, positions:, :] = jnp.where(new_row, entry[1:2, :], 0.0).astype(BF16)
    factor_ref[...] = jnp.broadcast_to(
        guidance_factor(sizes_ref, guidance_ref, factor_ref.shape[0]), factor_ref.shape
    )
    scores = jnp.concatenate(
        [
            lax.dot_general(wide[r], k_ref[r], NT, preferred_element_type=F32)
            for r in range(requests)
        ],
        axis=0,
    )
    scores = scores * SCALE
    heads = TOPK * H
    request_of_row = iota((requests * heads, 1), 0) // heads
    length = jnp.zeros((requests * heads, 1), jnp.int32)
    for r in range(requests):
        length = jnp.where(request_of_row == r, lengths_ref[0, r], length)
    column = iota(scores.shape, 1)
    live = (column < positions) & (block * positions + column < length)
    live = live | ((column == positions) & owner)
    top = jnp.max(jnp.where(live, scores, NEG), axis=1, keepdims=True)
    peaks = top.astype(BF16).astype(F32)
    weights = jnp.where(live, jnp.exp(scores - peaks), 0.0)
    totals = jnp.sum(weights, axis=1, keepdims=True)
    highs = totals.astype(BF16).astype(F32)
    lows = totals - highs
    weights = weights.astype(BF16)
    products = [dot(weights[r * heads : (r + 1) * heads], v_ref[r]) for r in range(requests)]
    sub = iota((8, LANES), 0)
    lane = iota((8, LANES), 1)
    for r in range(requests):
        at = slice(r * heads, (r + 1) * heads)
        values, peak, high, low = products[r], peaks[at], highs[at], lows[at]
        for k in range(TOPK):
            for quarter in range(H // HEADS_ROW):
                half, group = quarter // 2, quarter % 2
                base = k * H + (quarter // 2) * 8
                parts = []
                for j in range(HEADS_ROW):
                    head = quarter * HEADS_ROW + j
                    tile = values[base : base + 8, head * HD : (head + 1) * HD]
                    parts.append(jnp.sum(jnp.where(sub == head % 8, tile, 0.0), axis=0, keepdims=True))
                part = sub - group * HEADS_ROW
                here = (part >= 0) & (part < HEADS_ROW)
                stats = jnp.where(lane == part, peak[base : base + 8], 0.0)
                stats = stats + jnp.where(lane == part + 4, high[base : base + 8], 0.0)
                stats = stats + jnp.where(lane == part + 8, low[base : base + 8], 0.0)
                parts.append(jnp.sum(jnp.where(here, stats, 0.0), axis=0, keepdims=True))
                row = group * requests + r
                rows_ref[half, k, row : row + 1, :] = jnp.concatenate(parts, axis=1)
    request = iota((8, 1), 0) % requests
    chosen = []
    for k in range(TOPK):
        picked = jnp.zeros((8, 1), jnp.int32)
        for r in range(requests):
            picked = jnp.where(request == r, ids_ref[k, first_request + r], picked)
        chosen.append(picked)
    for plane in range(out_ref.shape[0]):
        expert, half = plane // 2, plane % 2
        message = jnp.where(chosen[0] == expert, rows_ref[half, 0], 0.0)
        message = message + jnp.where(chosen[1] == expert, rows_ref[half, 1], 0.0)
        out_ref[plane] = message.astype(BF16)


def spread_lanes(first_lane):
    rows, columns = iota((LANES, HEADS_ROW * HD), 0), iota((LANES, HEADS_ROW * HD), 1)
    return rows == first_lane + columns // HD


def merged(parts, stats, groups):
    count = stats.shape[0]
    peak = jnp.max(stats, axis=0)
    scale = jnp.exp(stats - peak[None])
    rows = count * groups * 8
    flat = scale.reshape(rows, LANES)
    high = flat.astype(BF16)
    low = (flat - high.astype(F32)).astype(BF16)
    lift = spread_lanes(0).astype(BF16)
    scales = dot(high, lift) + dot(low, lift)
    sums = dot(
        stats.reshape(rows, LANES).astype(BF16), (spread_lanes(4) | spread_lanes(8)).astype(BF16)
    )
    numerator, denominator = [], []
    for g in range(groups):
        top, bottom = 0.0, 0.0
        for n in range(count):
            at = (n * groups + g) * 8
            factor = scales[at : at + 8]
            top = top + parts(n, g) * factor
            bottom = bottom + sums[at : at + 8] * factor
        numerator.append(top)
        denominator.append(bottom)
    return numerator, denominator, peak


def merge_kernel(
    in_ref, weight_ref, first_gain_ref, second_gain_ref, out_ref, gains_ref
):
    gains_ref[0, :] = first_gain_ref[...].astype(F32)
    gains_ref[1, :] = second_gain_ref[...].astype(F32)
    wide = HEADS_ROW * HD
    copies = out_ref.shape[0]
    stats = in_ref[:, :, wide:].astype(F32)[:, None]
    numerator, denominator, peak = merged(
        lambda n, g: in_ref[n, :, :wide].astype(F32), stats, 1
    )
    lane = iota((8, LANES), 1)
    packed = jnp.where(lane < HEADS_ROW, peak[0], 0.0)
    for j in range(HEADS_ROW):
        total = denominator[0][:, j * HD : (j + 1) * HD]
        high = total.astype(BF16).astype(F32)
        packed = jnp.where(lane == 4 + j, high, packed)
        packed = jnp.where(lane == 8 + j, total - high, packed)
    blocks = [numerator[0][:, j * HD : (j + 1) * HD] for j in range(HEADS_ROW)] + [packed]
    blocks = [block.astype(BF16) for block in blocks]
    for copy in range(copies):
        for j, block in enumerate(blocks):
            out_ref[copy, j * 8 : (j + 1) * 8, :] = block
        out_ref[copy, len(blocks) * 8 :, :] = weight_ref[:, copy * LANES : (copy + 1) * LANES]


def project_kernel(in_ref, residual_ref, router_ref, ids_ref, out_ref, stats_ref, weight_ref):
    requests = 4
    columns, groups = 4, 4
    head_rows = HEADS_ROW * 8
    weight_rows = in_ref.shape[1] - head_rows - 8
    sources = in_ref.shape[0]
    expert = expert_of_plane()
    for source in range(sources):
        stats_ref[source] = in_ref[source, head_rows : head_rows + 8, :].astype(F32)
        weight_ref[source * weight_rows : (source + 1) * weight_rows, :] = in_ref[
            source, head_rows + 8 :, :
        ]
    stats = stats_ref[...].reshape(columns, groups, 8, LANES)

    def part(n, g):
        source = n * groups + g
        return jnp.concatenate(
            [in_ref[source, j * 8 : (j + 1) * 8, :] for j in range(HEADS_ROW)], axis=1
        ).astype(F32)

    numerator, denominator, _ = merged(part, stats, groups)
    inputs = residual_ref[0].astype(F32)
    normed = (inputs * rms(inputs)).astype(BF16)
    logits = lax.dot_general(router_ref[...], normed, NT, preferred_element_type=F32)
    row = iota((8 * groups, 1), 0)
    gate = share_column(logits, ids_ref, expert, row // 8 * requests + row % requests)
    attended = jnp.concatenate(
        [top / jnp.maximum(bottom, 1e-30) for top, bottom in zip(numerator, denominator)], axis=0
    )
    gated = (attended.astype(BF16).astype(F32) * gate).astype(BF16)
    wide = HEADS_ROW * HD
    lower = dot(gated, weight_ref[:wide, :])
    upper = dot(gated, weight_ref[wide:, :])
    mixed = jnp.where(row % 8 < requests, lower, upper)
    sub = iota((8, LANES), 0)
    tiles = []
    for g in range(groups):
        tile = mixed[g * 8 : (g + 1) * 8]
        tiles.append(tile + pltpu.roll(tile, 4, 0))
    for pair in range(groups // 2):
        both = jnp.where(sub < requests, tiles[2 * pair], tiles[2 * pair + 1]).astype(BF16)
        for copy in range(out_ref.shape[0]):
            out_ref[copy, pair * 8 : (pair + 1) * 8, :] = both


def fold_kernel(in_ref, out_ref):
    total = in_ref[0].astype(F32)
    for n in range(1, in_ref.shape[0]):
        total = total + in_ref[n].astype(F32)
    total = total.astype(BF16)
    for copy in range(out_ref.shape[0]):
        out_ref[copy] = total


def expert_kernel(
    in_ref, residual_ref, gain_ref, router_ref, ids_ref, gate_ref, up_ref, down_ref, out_ref
):
    chunks = in_ref.shape[0]
    requests = in_ref.shape[1]
    middle = jnp.concatenate(
        [
            residual_ref[0, :, chunk * LANES : (chunk + 1) * LANES].astype(F32)
            + in_ref[chunk].astype(F32)
            for chunk in range(chunks)
        ],
        axis=1,
    )
    inputs = (middle * rms(middle) * gain_ref[0:1, :]).astype(BF16)
    logits = lax.dot_general(router_ref[...], inputs, NT, preferred_element_type=F32)
    share = share_column(logits, ids_ref, expert_of_plane(), iota((requests, 1), 0))
    gate = lax.dot_general(inputs, gate_ref[...], NT, preferred_element_type=F32)
    up = lax.dot_general(inputs, up_ref[...], NT, preferred_element_type=F32)
    hidden = (gate / (1.0 + jnp.exp(-gate)) * up * share).astype(BF16)
    out = dot(hidden, down_ref[...])
    for chunk in range(chunks):
        out_ref[chunk] = out[:, chunk * LANES : (chunk + 1) * LANES].astype(BF16)


def finish_kernel(in_ref, attention_ref, residual_ref, out_ref):
    total = attention_ref[0].astype(F32)
    for n in range(1, attention_ref.shape[0]):
        total = total + attention_ref[n].astype(F32)
    for n in range(in_ref.shape[0]):
        total = total + in_ref[n].astype(F32)
    chunk = lax.axis_index("x") * lax.axis_size("req") + lax.axis_index("req")
    at = pl.ds(pl.multiple_of(chunk * LANES, LANES), LANES)
    total = (total + residual_ref[0, :, at].astype(F32)).astype(out_ref.dtype)
    half = out_ref.shape[1]
    copies = out_ref.shape[0] // 2
    for stream in range(2):
        for copy in range(copies):
            out_ref[stream * copies + copy] = total[stream * half : (stream + 1) * half]


def head_kernel(in_ref, gain_ref, words_ref, factor_ref, out_ref):
    half = in_ref.shape[1]
    chunks = in_ref.shape[0] // 2
    joined = jnp.concatenate(
        [
            jnp.concatenate(
                [in_ref[stream * chunks + chunk].astype(F32) for chunk in range(chunks)], axis=1
            )
            for stream in range(2)
        ],
        axis=0,
    )
    inputs = (joined * gain_ref[1:2, :]).astype(BF16)
    logits = lax.dot_general(inputs, words_ref[...], NT, preferred_element_type=F32)
    logits = logits * rms(joined)
    factor = factor_ref[:, :1]
    conditional, unconditional = logits[:half], logits[half:]
    out_ref[...] = unconditional + factor * (conditional - unconditional)


def exchanged(value, axis):
    return lax.all_to_all(value, axis, 0, 0, tiled=True)


def local(
    residual,
    queries,
    new_entries,
    key_cache,
    value_cache,
    lengths,
    attention_ids,
    expert_ids,
    attention_router,
    expert_router,
    attention_output,
    expert_gain,
    expert_gate,
    expert_up,
    expert_down,
    final_gain,
    unembedding,
    tenant_sizes,
    guidance,
):
    planes = lax.axis_size("z")
    plane = ("x", "req")
    members = lax.axis_size(plane)
    requests = residual.shape[1]
    shape = jax.ShapeDtypeStruct

    rows, positions = key_cache.shape[1:3]
    partial, factor, ids = call(
        attend_kernel,
        (
            shape((planes, 8, ROW), BF16),
            shape((requests // 2, LANES), F32),
            shape(expert_ids.shape[::-1], jnp.int32),
        ),
        [hbm()] * 9,
        [
            pltpu.VMEM(queries.shape, BF16),
            pltpu.VMEM((rows, positions + SPARE, D), BF16),
            pltpu.VMEM((rows, positions + SPARE, D), BF16),
            pltpu.VMEM(new_entries.shape, BF16),
            pltpu.SMEM(lengths.shape, jnp.int32),
            pltpu.SMEM(attention_ids.shape[::-1], jnp.int32),
            pltpu.SMEM(tenant_sizes.shape, jnp.int32),
            pltpu.SMEM(guidance.shape, jnp.int32),
            pltpu.VMEM((2, TOPK, 8, ROW), F32),
            pltpu.SemaphoreType.DMA((7,)),
            pltpu.SemaphoreType.DMA((2,)),
        ],
    )(
        *(
            pltpu.with_memory_space_constraint(operand, pltpu.HBM)
            for operand in (
                queries,
                key_cache,
                value_cache,
                new_entries,
                lengths,
                attention_ids.T,
                tenant_sizes,
                guidance,
                expert_ids.T,
            )
        )
    )
    partial = exchanged(partial, "z")

    weight_rows = attention_output.shape[0]
    merged_rows = HEADS_ROW * 8 + 8 + weight_rows
    both, gains = call(
        merge_kernel,
        (shape((members, merged_rows, LANES), BF16), shape((2, D), F32)),
        [vmem()] * 4,
    )(partial, attention_output, expert_gain, final_gain)
    both = exchanged(both, plane)

    chunk = shape((planes, requests, LANES), BF16)
    projected = call(
        project_kernel,
        chunk,
        [vmem()] * 4,
        [pltpu.VMEM((members, 8, LANES), F32), pltpu.VMEM((members * weight_rows, LANES), BF16)],
    )(both, residual, attention_router.T, attention_ids.T)
    projected = exchanged(projected, "z")

    spread = shape((members, requests, LANES), BF16)
    attention = call(fold_kernel, spread, [vmem()])(projected)
    attention = exchanged(attention, plane)

    hidden = call(expert_kernel, spread, [vmem()] * 8)(
        attention,
        residual,
        gains,
        expert_router.T,
        ids,
        expert_gate,
        expert_up,
        expert_down,
    )
    hidden = exchanged(hidden, plane)
    hidden = call(fold_kernel, chunk, [vmem()])(hidden)
    hidden = exchanged(hidden, "z")

    streams = lax.axis_size("cfg")
    final = call(
        finish_kernel, shape((streams * members, requests // 2, LANES), BF16), [vmem()] * 3
    )(hidden, projected, residual)
    final = exchanged(final, ("cfg",) + plane)

    return call(
        head_kernel,
        shape((requests // 2, unembedding.shape[0]), F32),
        [vmem()] * 4,
    )(final, gains, unembedding, factor)


def solution(mesh):
    sizes = mesh.devices.shape
    split = Mesh(mesh.devices.reshape(sizes[0], 16, sizes[1] // 16, sizes[2]), ("cfg", "z", "x", "req"))
    blk = ("z", "x")
    rows = P(("z", "x", "req"), None)
    placed = (
        P("cfg", None, None),
        P("cfg", "req", None),
        P("cfg", "req", None, None),
        P("cfg", "req", blk, None),
        P("cfg", "req", blk, None),
        P("cfg", "req"),
        P(),
        P(),
        P(),
        P(),
        rows,
        P(),
        rows,
        rows,
        rows,
        P(),
        rows,
        P(),
        P(),
    )
    return jax.shard_map(
        local,
        mesh=split,
        in_specs=placed,
        out_specs=P("cfg", ("z", "x", "req")),
        check_vma=False,
    )
```

```python
import math

import jax
import jax.numpy as jnp
from jax import lax
from jax.experimental import pallas as pl
from jax.experimental.pallas import tpu as pltpu
from jax.sharding import Mesh
from jax.sharding import PartitionSpec as P

D = 2048
H = 16
HD = 128
FF = 5632
TOPK = 2
EPS = 1e-05
NEG = -1e30
SPARE = 16
LANES = 128
HEADS_ROW = 4
ROW = HEADS_ROW * HD + LANES
SCALE = 1.0 / math.sqrt(HD)

F32 = jnp.float32
BF16 = jnp.bfloat16
NT = (((1,), (1,)), ((), ()))


def vmem():
    return pl.BlockSpec(memory_space=pltpu.VMEM)


def hbm():
    return pl.BlockSpec(memory_space=pltpu.HBM)


def call(body, outs, specs, scratch=()):
    return pl.pallas_call(
        body,
        out_shape=outs,
        in_specs=specs,
        out_specs=jax.tree.map(lambda _: vmem(), outs),
        scratch_shapes=list(scratch),
        compiler_params=pltpu.CompilerParams(vmem_limit_bytes=48 * 1024 * 1024),
    )


def iota(shape, dim):
    return lax.broadcasted_iota(jnp.int32, shape, dim)


def dot(a, b):
    return jnp.dot(a, b, preferred_element_type=F32)


def rms(values):
    return lax.rsqrt(jnp.mean(values * values, axis=-1, keepdims=True) + EPS)


def expert_of_plane():
    return lax.axis_index("z") // 2


def share_column(logits_t, ids_ref, expert, lane_of_row):
    experts = iota(logits_t.shape, 0)
    first_id, second_id = ids_ref[0:1, :], ids_ref[1:2, :]
    first = jnp.sum(jnp.where(experts == first_id, logits_t, 0.0), axis=0, keepdims=True)
    second = jnp.sum(jnp.where(experts == second_id, logits_t, 0.0), axis=0, keepdims=True)
    gate_first = 1.0 / (1.0 + jnp.exp(second - first))
    gate_second = 1.0 / (1.0 + jnp.exp(first - second))
    share = jnp.where(first_id == expert, gate_first, 0.0) + jnp.where(
        second_id == expert, gate_second, 0.0
    )
    lanes = iota((lane_of_row.shape[0], share.shape[1]), 1)
    return jnp.sum(jnp.where(lanes == lane_of_row, share, 0.0), axis=1, keepdims=True)


def guidance_factor(sizes_ref, guidance_ref, half):
    request = lax.axis_index("cfg") * half + iota((half, 1), 0)
    tenants = sizes_ref.shape[0]
    tenant = jnp.zeros((half, 1), jnp.int32)
    end = 0
    for t in range(tenants):
        end = end + sizes_ref[t]
        tenant = tenant + (request >= end).astype(jnp.int32)
    chosen = jnp.zeros((half, 1), jnp.int32)
    for t in range(tenants):
        chosen = jnp.where(tenant == t, guidance_ref[t], chosen)
    return chosen.astype(F32) / 4.0


def attend_kernel(
    q_hbm,
    k_hbm,
    v_hbm,
    new_hbm,
    lengths_hbm,
    ids_hbm,
    sizes_hbm,
    guidance_hbm,
    expert_ids_hbm,
    out_ref,
    factor_ref,
    expert_ids_ref,
    q_ref,
    k_ref,
    v_ref,
    new_ref,
    lengths_ref,
    ids_ref,
    sizes_ref,
    guidance_ref,
    rows_ref,
    small_sems,
    cache_sems,
):
    requests, positions = k_hbm.shape[1], k_hbm.shape[2]
    small = [
        pltpu.make_async_copy(source, target, small_sems.at[n])
        for n, (source, target) in enumerate(
            [
                (q_hbm, q_ref),
                (new_hbm, new_ref),
                (lengths_hbm, lengths_ref),
                (ids_hbm, ids_ref),
                (sizes_hbm, sizes_ref),
                (guidance_hbm, guidance_ref),
                (expert_ids_hbm, expert_ids_ref),
            ]
        )
    ]
    keys = pltpu.make_async_copy(k_hbm.at[0], k_ref.at[:, :positions], cache_sems.at[0])
    values_in = pltpu.make_async_copy(v_hbm.at[0], v_ref.at[:, :positions], cache_sems.at[1])
    keys.start()
    values_in.start()
    for copy in small:
        copy.start()
    block = lax.axis_index("z") * lax.axis_size("x") + lax.axis_index("x")
    owner = block == 0
    first_request = lax.axis_index("req") * requests
    own_head = iota((H, D), 0) == iota((H, D), 1) // HD
    for copy in [*small, keys, values_in]:
        copy.wait()
    queries = q_ref[0].astype(F32)
    wide = [
        jnp.concatenate(
            [
                jnp.where(own_head, queries[r : r + 1, k * D : (k + 1) * D], 0.0)
                for k in range(TOPK)
            ],
            axis=0,
        ).astype(BF16)
        for r in range(requests)
    ]
    new_row = (iota((SPARE, D), 0) == 0) & owner
    for r in range(requests):
        entry = new_ref[0, r].astype(F32)
        k_ref[r, positions:, :] = jnp.where(new_row, entry[0:1, :], 0.0).astype(BF16)
        v_ref[r, positions:, :] = jnp.where(new_row, entry[1:2, :], 0.0).astype(BF16)
    factor_ref[...] = jnp.broadcast_to(
        guidance_factor(sizes_ref, guidance_ref, factor_ref.shape[0]), factor_ref.shape
    )
    scores = jnp.concatenate(
        [
            lax.dot_general(wide[r], k_ref[r], NT, preferred_element_type=F32)
            for r in range(requests)
        ],
        axis=0,
    )
    scores = scores * SCALE
    heads = TOPK * H
    request_of_row = iota((requests * heads, 1), 0) // heads
    length = jnp.zeros((requests * heads, 1), jnp.int32)
    for r in range(requests):
        length = jnp.where(request_of_row == r, lengths_ref[0, r], length)
    column = iota(scores.shape, 1)
    live = (column < positions) & (block * positions + column < length)
    live = live | ((column == positions) & owner)
    top = jnp.max(jnp.where(live, scores, NEG), axis=1, keepdims=True)
    peaks = top.astype(BF16).astype(F32)
    weights = jnp.where(live, jnp.exp(scores - peaks), 0.0)
    totals = jnp.sum(weights, axis=1, keepdims=True)
    highs = totals.astype(BF16).astype(F32)
    lows = totals - highs
    weights = weights.astype(BF16)
    products = [dot(weights[r * heads : (r + 1) * heads], v_ref[r]) for r in range(requests)]
    sub = iota((8, LANES), 0)
    lane = iota((8, LANES), 1)
    for r in range(requests):
        at = slice(r * heads, (r + 1) * heads)
        values, peak, high, low = products[r], peaks[at], highs[at], lows[at]
        for k in range(TOPK):
            for quarter in range(H // HEADS_ROW):
                half, group = quarter // 2, quarter % 2
                base = k * H + (quarter // 2) * 8
                parts = []
                for j in range(HEADS_ROW):
                    head = quarter * HEADS_ROW + j
                    tile = values[base : base + 8, head * HD : (head + 1) * HD]
                    parts.append(jnp.sum(jnp.where(sub == head % 8, tile, 0.0), axis=0, keepdims=True))
                part = sub - group * HEADS_ROW
                here = (part >= 0) & (part < HEADS_ROW)
                stats = jnp.where(lane == part, peak[base : base + 8], 0.0)
                stats = stats + jnp.where(lane == part + 4, high[base : base + 8], 0.0)
                stats = stats + jnp.where(lane == part + 8, low[base : base + 8], 0.0)
                parts.append(jnp.sum(jnp.where(here, stats, 0.0), axis=0, keepdims=True))
                row = group * requests + r
                rows_ref[half, k, row : row + 1, :] = jnp.concatenate(parts, axis=1)
    request = iota((8, 1), 0) % requests
    chosen = []
    for k in range(TOPK):
        picked = jnp.zeros((8, 1), jnp.int32)
        for r in range(requests):
            picked = jnp.where(request == r, ids_ref[k, first_request + r], picked)
        chosen.append(picked)
    for plane in range(out_ref.shape[0]):
        expert, half = plane // 2, plane % 2
        message = jnp.where(chosen[0] == expert, rows_ref[half, 0], 0.0)
        message = message + jnp.where(chosen[1] == expert, rows_ref[half, 1], 0.0)
        out_ref[plane] = message.astype(BF16)


def spread_lanes(first_lane):
    rows, columns = iota((LANES, HEADS_ROW * HD), 0), iota((LANES, HEADS_ROW * HD), 1)
    return rows == first_lane + columns // HD


def merged(parts, stats, groups):
    count = stats.shape[0]
    peak = jnp.max(stats, axis=0)
    scale = jnp.exp(stats - peak[None])
    rows = count * groups * 8
    flat = scale.reshape(rows, LANES)
    high = flat.astype(BF16)
    low = (flat - high.astype(F32)).astype(BF16)
    lift = spread_lanes(0).astype(BF16)
    scales = dot(high, lift) + dot(low, lift)
    sums = dot(
        stats.reshape(rows, LANES).astype(BF16), (spread_lanes(4) | spread_lanes(8)).astype(BF16)
    )
    numerator, denominator = [], []
    for g in range(groups):
        top, bottom = 0.0, 0.0
        for n in range(count):
            at = (n * groups + g) * 8
            factor = scales[at : at + 8]
            top = top + parts(n, g) * factor
            bottom = bottom + sums[at : at + 8] * factor
        numerator.append(top)
        denominator.append(bottom)
    return numerator, denominator, peak


def merge_kernel(
    in_ref, weight_ref, first_gain_ref, second_gain_ref, out_ref, gains_ref
):
    gains_ref[0, :] = first_gain_ref[...].astype(F32)
    gains_ref[1, :] = second_gain_ref[...].astype(F32)
    wide = HEADS_ROW * HD
    copies = out_ref.shape[0]
    stats = in_ref[:, :, wide:].astype(F32)[:, None]
    numerator, denominator, peak = merged(
        lambda n, g: in_ref[n, :, :wide].astype(F32), stats, 1
    )
    lane = iota((8, LANES), 1)
    packed = jnp.where(lane < HEADS_ROW, peak[0], 0.0)
    for j in range(HEADS_ROW):
        total = denominator[0][:, j * HD : (j + 1) * HD]
        high = total.astype(BF16).astype(F32)
        packed = jnp.where(lane == 4 + j, high, packed)
        packed = jnp.where(lane == 8 + j, total - high, packed)
    blocks = [numerator[0][:, j * HD : (j + 1) * HD] for j in range(HEADS_ROW)] + [packed]
    blocks = [block.astype(BF16) for block in blocks]
    for copy in range(copies):
        for j, block in enumerate(blocks):
            out_ref[copy, j * 8 : (j + 1) * 8, :] = block
        out_ref[copy, len(blocks) * 8 :, :] = weight_ref[:, copy * LANES : (copy + 1) * LANES]


def project_kernel(in_ref, residual_ref, router_ref, ids_ref, out_ref, stats_ref, weight_ref):
    requests = 4
    columns, groups = 4, 4
    head_rows = HEADS_ROW * 8
    weight_rows = in_ref.shape[1] - head_rows - 8
    sources = in_ref.shape[0]
    expert = expert_of_plane()
    for source in range(sources):
        place = source % columns * groups + source // columns
        stats_ref[place] = in_ref[source, head_rows : head_rows + 8, :].astype(F32)
        weight_ref[place * weight_rows : (place + 1) * weight_rows, :] = in_ref[
            source, head_rows + 8 :, :
        ]
    stats = stats_ref[...].reshape(columns, groups, 8, LANES)

    def part(n, g):
        source = g * columns + n
        return jnp.concatenate(
            [in_ref[source, j * 8 : (j + 1) * 8, :] for j in range(HEADS_ROW)], axis=1
        ).astype(F32)

    numerator, denominator, _ = merged(part, stats, groups)
    inputs = residual_ref[0].astype(F32)
    normed = (inputs * rms(inputs)).astype(BF16)
    logits = lax.dot_general(router_ref[...], normed, NT, preferred_element_type=F32)
    row = iota((8 * groups, 1), 0)
    gate = share_column(logits, ids_ref, expert, row // 8 * requests + row % requests)
    attended = jnp.concatenate(
        [top / jnp.maximum(bottom, 1e-30) for top, bottom in zip(numerator, denominator)], axis=0
    )
    gated = (attended.astype(BF16).astype(F32) * gate).astype(BF16)
    wide = HEADS_ROW * HD
    lower = dot(gated, weight_ref[:wide, :])
    upper = dot(gated, weight_ref[wide:, :])
    mixed = jnp.where(row % 8 < requests, lower, upper)
    sub = iota((8, LANES), 0)
    tiles = []
    for g in range(groups):
        tile = mixed[g * 8 : (g + 1) * 8]
        tiles.append(tile + pltpu.roll(tile, 4, 0))
    for pair in range(groups // 2):
        both = jnp.where(sub < requests, tiles[2 * pair], tiles[2 * pair + 1]).astype(BF16)
        for copy in range(out_ref.shape[0]):
            out_ref[copy, pair * 8 : (pair + 1) * 8, :] = both


def fold_kernel(in_ref, out_ref):
    total = in_ref[0].astype(F32)
    for n in range(1, in_ref.shape[0]):
        total = total + in_ref[n].astype(F32)
    total = total.astype(BF16)
    for copy in range(out_ref.shape[0]):
        out_ref[copy] = total


def expert_kernel(
    in_ref, residual_ref, gain_ref, router_ref, ids_ref, gate_ref, up_ref, down_ref, out_ref
):
    chunks = in_ref.shape[0]
    requests = in_ref.shape[1]
    middle = jnp.concatenate(
        [
            residual_ref[0, :, chunk * LANES : (chunk + 1) * LANES].astype(F32)
            + in_ref[chunk].astype(F32)
            for chunk in range(chunks)
        ],
        axis=1,
    )
    inputs = (middle * rms(middle) * gain_ref[0:1, :]).astype(BF16)
    logits = lax.dot_general(router_ref[...], inputs, NT, preferred_element_type=F32)
    share = share_column(logits, ids_ref, expert_of_plane(), iota((requests, 1), 0))
    gate = lax.dot_general(inputs, gate_ref[...], NT, preferred_element_type=F32)
    up = lax.dot_general(inputs, up_ref[...], NT, preferred_element_type=F32)
    hidden = (gate / (1.0 + jnp.exp(-gate)) * up * share).astype(BF16)
    out = dot(hidden, down_ref[...])
    for chunk in range(chunks):
        out_ref[chunk] = out[:, chunk * LANES : (chunk + 1) * LANES].astype(BF16)


def finish_kernel(in_ref, attention_ref, residual_ref, out_ref):
    total = attention_ref[0].astype(F32)
    for n in range(1, attention_ref.shape[0]):
        total = total + attention_ref[n].astype(F32)
    for n in range(in_ref.shape[0]):
        total = total + in_ref[n].astype(F32)
    chunk = lax.axis_index("req") * lax.axis_size("x") + lax.axis_index("x")
    at = pl.ds(pl.multiple_of(chunk * LANES, LANES), LANES)
    total = (total + residual_ref[0, :, at].astype(F32)).astype(out_ref.dtype)
    half = out_ref.shape[1]
    copies = out_ref.shape[0] // 2
    for stream in range(2):
        for copy in range(copies):
            out_ref[stream * copies + copy] = total[stream * half : (stream + 1) * half]


def head_kernel(in_ref, gain_ref, words_ref, factor_ref, out_ref):
    half = in_ref.shape[1]
    chunks = in_ref.shape[0] // 2
    joined = jnp.concatenate(
        [
            jnp.concatenate(
                [in_ref[stream * chunks + chunk].astype(F32) for chunk in range(chunks)], axis=1
            )
            for stream in range(2)
        ],
        axis=0,
    )
    inputs = (joined * gain_ref[1:2, :]).astype(BF16)
    logits = lax.dot_general(inputs, words_ref[...], NT, preferred_element_type=F32)
    logits = logits * rms(joined)
    factor = factor_ref[:, :1]
    conditional, unconditional = logits[:half], logits[half:]
    out_ref[...] = unconditional + factor * (conditional - unconditional)


def exchanged(value, axis):
    return lax.all_to_all(value, axis, 0, 0, tiled=True)


def local(
    residual,
    queries,
    new_entries,
    key_cache,
    value_cache,
    lengths,
    attention_ids,
    expert_ids,
    attention_router,
    expert_router,
    attention_output,
    expert_gain,
    expert_gate,
    expert_up,
    expert_down,
    final_gain,
    unembedding,
    tenant_sizes,
    guidance,
):
    planes = lax.axis_size("z")
    plane = ("req", "x")
    members = lax.axis_size(plane)
    requests = residual.shape[1]
    shape = jax.ShapeDtypeStruct

    rows, positions = key_cache.shape[1:3]
    partial, factor, ids = call(
        attend_kernel,
        (
            shape((planes, 8, ROW), BF16),
            shape((requests // 2, LANES), F32),
            shape(expert_ids.shape[::-1], jnp.int32),
        ),
        [hbm()] * 9,
        [
            pltpu.VMEM(queries.shape, BF16),
            pltpu.VMEM((rows, positions + SPARE, D), BF16),
            pltpu.VMEM((rows, positions + SPARE, D), BF16),
            pltpu.VMEM(new_entries.shape, BF16),
            pltpu.SMEM(lengths.shape, jnp.int32),
            pltpu.SMEM(attention_ids.shape[::-1], jnp.int32),
            pltpu.SMEM(tenant_sizes.shape, jnp.int32),
            pltpu.SMEM(guidance.shape, jnp.int32),
            pltpu.VMEM((2, TOPK, 8, ROW), F32),
            pltpu.SemaphoreType.DMA((7,)),
            pltpu.SemaphoreType.DMA((2,)),
        ],
    )(
        *(
            pltpu.with_memory_space_constraint(operand, pltpu.HBM)
            for operand in (
                queries,
                key_cache,
                value_cache,
                new_entries,
                lengths,
                attention_ids.T,
                tenant_sizes,
                guidance,
                expert_ids.T,
            )
        )
    )
    partial = exchanged(partial, "z")

    weight_rows = attention_output.shape[0]
    merged_rows = HEADS_ROW * 8 + 8 + weight_rows
    both, gains = call(
        merge_kernel,
        (shape((members, merged_rows, LANES), BF16), shape((2, D), F32)),
        [vmem()] * 4,
    )(partial, attention_output, expert_gain, final_gain)
    both = exchanged(both, plane)

    chunk = shape((planes, requests, LANES), BF16)
    projected = call(
        project_kernel,
        chunk,
        [vmem()] * 4,
        [pltpu.VMEM((members, 8, LANES), F32), pltpu.VMEM((members * weight_rows, LANES), BF16)],
    )(both, residual, attention_router.T, attention_ids.T)
    projected = exchanged(projected, "z")

    spread = shape((members, requests, LANES), BF16)
    attention = call(fold_kernel, spread, [vmem()])(projected)
    attention = exchanged(attention, plane)

    hidden = call(expert_kernel, spread, [vmem()] * 8)(
        attention,
        residual,
        gains,
        expert_router.T,
        ids,
        expert_gate,
        expert_up,
        expert_down,
    )
    hidden = exchanged(hidden, plane)
    hidden = call(fold_kernel, chunk, [vmem()])(hidden)
    hidden = exchanged(hidden, "z")

    streams = lax.axis_size("cfg")
    final = call(
        finish_kernel, shape((streams * members, requests // 2, LANES), BF16), [vmem()] * 3
    )(hidden, projected, residual)
    final = exchanged(final, ("cfg",) + plane)

    return call(
        head_kernel,
        shape((requests // 2, unembedding.shape[0]), F32),
        [vmem()] * 4,
    )(final, gains, unembedding, factor)


def solution(mesh):
    sizes = mesh.devices.shape
    split = Mesh(mesh.devices.reshape(sizes[0], 16, sizes[1] // 16, sizes[2]), ("cfg", "z", "x", "req"))
    blk = ("z", "x")
    rows = P(("z", "x", "req"), None)
    placed = (
        P("cfg", None, None),
        P("cfg", "req", None),
        P("cfg", "req", None, None),
        P("cfg", "req", blk, None),
        P("cfg", "req", blk, None),
        P("cfg", "req"),
        P(),
        P(),
        P(),
        P(),
        rows,
        P(),
        rows,
        rows,
        rows,
        P(),
        rows,
        P(),
        P(),
    )
    return jax.shard_map(
        local,
        mesh=split,
        in_specs=placed,
        out_specs=P("cfg", ("z", "x", "req")),
        check_vma=False,
    )
```

```python
import math

import jax
import jax.numpy as jnp
from jax import lax
from jax.experimental import pallas as pl
from jax.experimental.pallas import tpu as pltpu
from jax.sharding import Mesh
from jax.sharding import PartitionSpec as P

D = 2048
H = 16
HD = 128
FF = 5632
TOPK = 2
EPS = 1e-05
NEG = -1e30
SPARE = 16
LANES = 128
HEADS_ROW = 4
ROW = HEADS_ROW * HD + LANES
SCALE = 1.0 / math.sqrt(HD)

F32 = jnp.float32
BF16 = jnp.bfloat16
NT = (((1,), (1,)), ((), ()))


def vmem():
    return pl.BlockSpec(memory_space=pltpu.VMEM)


def hbm():
    return pl.BlockSpec(memory_space=pltpu.HBM)


def call(body, outs, specs, scratch=()):
    return pl.pallas_call(
        body,
        out_shape=outs,
        in_specs=specs,
        out_specs=jax.tree.map(lambda _: vmem(), outs),
        scratch_shapes=list(scratch),
        compiler_params=pltpu.CompilerParams(vmem_limit_bytes=48 * 1024 * 1024),
    )


def iota(shape, dim):
    return lax.broadcasted_iota(jnp.int32, shape, dim)


def dot(a, b):
    return jnp.dot(a, b, preferred_element_type=F32)


def rms(values):
    return lax.rsqrt(jnp.mean(values * values, axis=-1, keepdims=True) + EPS)


def expert_of_plane():
    return lax.axis_index("z") // 2


def share_column(logits_t, ids_ref, expert, lane_of_row):
    experts = iota(logits_t.shape, 0)
    first_id, second_id = ids_ref[0:1, :], ids_ref[1:2, :]
    first = jnp.sum(jnp.where(experts == first_id, logits_t, 0.0), axis=0, keepdims=True)
    second = jnp.sum(jnp.where(experts == second_id, logits_t, 0.0), axis=0, keepdims=True)
    gate_first = 1.0 / (1.0 + jnp.exp(second - first))
    gate_second = 1.0 / (1.0 + jnp.exp(first - second))
    share = jnp.where(first_id == expert, gate_first, 0.0) + jnp.where(
        second_id == expert, gate_second, 0.0
    )
    lanes = iota((lane_of_row.shape[0], share.shape[1]), 1)
    return jnp.sum(jnp.where(lanes == lane_of_row, share, 0.0), axis=1, keepdims=True)


def guidance_factor(sizes_ref, guidance_ref, half):
    request = lax.axis_index("cfg") * half + iota((half, 1), 0)
    tenants = sizes_ref.shape[0]
    tenant = jnp.zeros((half, 1), jnp.int32)
    end = 0
    for t in range(tenants):
        end = end + sizes_ref[t]
        tenant = tenant + (request >= end).astype(jnp.int32)
    chosen = jnp.zeros((half, 1), jnp.int32)
    for t in range(tenants):
        chosen = jnp.where(tenant == t, guidance_ref[t], chosen)
    return chosen.astype(F32) / 4.0


def attend_kernel(
    q_hbm,
    k_hbm,
    v_hbm,
    new_hbm,
    lengths_hbm,
    ids_hbm,
    sizes_hbm,
    guidance_hbm,
    expert_ids_hbm,
    out_ref,
    factor_ref,
    expert_ids_ref,
    q_ref,
    k_ref,
    v_ref,
    new_ref,
    lengths_ref,
    ids_ref,
    sizes_ref,
    guidance_ref,
    rows_ref,
    small_sems,
    cache_sems,
):
    requests, positions = k_hbm.shape[1], k_hbm.shape[2]
    small = [
        pltpu.make_async_copy(source, target, small_sems.at[n])
        for n, (source, target) in enumerate(
            [
                (q_hbm, q_ref),
                (new_hbm, new_ref),
                (lengths_hbm, lengths_ref),
                (ids_hbm, ids_ref),
                (sizes_hbm, sizes_ref),
                (guidance_hbm, guidance_ref),
                (expert_ids_hbm, expert_ids_ref),
            ]
        )
    ]
    keys = pltpu.make_async_copy(k_hbm.at[0], k_ref.at[:, :positions], cache_sems.at[0])
    values_in = pltpu.make_async_copy(v_hbm.at[0], v_ref.at[:, :positions], cache_sems.at[1])
    keys.start()
    values_in.start()
    for copy in small:
        copy.start()
    block = lax.axis_index("z") * lax.axis_size("x") + lax.axis_index("x")
    owner = block == 0
    first_request = lax.axis_index("req") * requests
    own_head = iota((H, D), 0) == iota((H, D), 1) // HD
    for copy in [*small, keys, values_in]:
        copy.wait()
    queries = q_ref[0].astype(F32)
    wide = [
        jnp.concatenate(
            [
                jnp.where(own_head, queries[r : r + 1, k * D : (k + 1) * D], 0.0)
                for k in range(TOPK)
            ],
            axis=0,
        ).astype(BF16)
        for r in range(requests)
    ]
    new_row = (iota((SPARE, D), 0) == 0) & owner
    for r in range(requests):
        entry = new_ref[0, r].astype(F32)
        k_ref[r, positions:, :] = jnp.where(new_row, entry[0:1, :], 0.0).astype(BF16)
        v_ref[r, positions:, :] = jnp.where(new_row, entry[1:2, :], 0.0).astype(BF16)
    factor_ref[...] = jnp.broadcast_to(
        guidance_factor(sizes_ref, guidance_ref, factor_ref.shape[0]), factor_ref.shape
    )
    scores = jnp.concatenate(
        [
            lax.dot_general(wide[r], k_ref[r], NT, preferred_element_type=F32)
            for r in range(requests)
        ],
        axis=0,
    )
    scores = scores * SCALE
    heads = TOPK * H
    request_of_row = iota((requests * heads, 1), 0) // heads
    length = jnp.zeros((requests * heads, 1), jnp.int32)
    for r in range(requests):
        length = jnp.where(request_of_row == r, lengths_ref[0, r], length)
    column = iota(scores.shape, 1)
    live = (column < positions) & (block * positions + column < length)
    live = live | ((column == positions) & owner)
    top = jnp.max(jnp.where(live, scores, NEG), axis=1, keepdims=True)
    peaks = top.astype(BF16).astype(F32)
    weights = jnp.where(live, jnp.exp(scores - peaks), 0.0)
    totals = jnp.sum(weights, axis=1, keepdims=True)
    highs = totals.astype(BF16).astype(F32)
    lows = totals - highs
    weights = weights.astype(BF16)
    products = [dot(weights[r * heads : (r + 1) * heads], v_ref[r]) for r in range(requests)]
    sub = iota((8, LANES), 0)
    lane = iota((8, LANES), 1)
    for r in range(requests):
        at = slice(r * heads, (r + 1) * heads)
        values, peak, high, low = products[r], peaks[at], highs[at], lows[at]
        for k in range(TOPK):
            for quarter in range(H // HEADS_ROW):
                half, group = quarter // 2, quarter % 2
                base = k * H + (quarter // 2) * 8
                parts = []
                for j in range(HEADS_ROW):
                    head = quarter * HEADS_ROW + j
                    tile = values[base : base + 8, head * HD : (head + 1) * HD]
                    parts.append(jnp.sum(jnp.where(sub == head % 8, tile, 0.0), axis=0, keepdims=True))
                part = sub - group * HEADS_ROW
                here = (part >= 0) & (part < HEADS_ROW)
                stats = jnp.where(lane == part, peak[base : base + 8], 0.0)
                stats = stats + jnp.where(lane == part + 4, high[base : base + 8], 0.0)
                stats = stats + jnp.where(lane == part + 8, low[base : base + 8], 0.0)
                parts.append(jnp.sum(jnp.where(here, stats, 0.0), axis=0, keepdims=True))
                row = group * requests + r
                rows_ref[half, k, row : row + 1, :] = jnp.concatenate(parts, axis=1)
    request = iota((8, 1), 0) % requests
    chosen = []
    for k in range(TOPK):
        picked = jnp.zeros((8, 1), jnp.int32)
        for r in range(requests):
            picked = jnp.where(request == r, ids_ref[k, first_request + r], picked)
        chosen.append(picked)
    for plane in range(out_ref.shape[0]):
        expert, half = plane // 2, plane % 2
        message = jnp.where(chosen[0] == expert, rows_ref[half, 0], 0.0)
        message = message + jnp.where(chosen[1] == expert, rows_ref[half, 1], 0.0)
        out_ref[plane] = message.astype(BF16)


def spread_lanes(first_lane):
    rows, columns = iota((LANES, HEADS_ROW * HD), 0), iota((LANES, HEADS_ROW * HD), 1)
    return rows == first_lane + columns // HD


def merged(parts, stats, groups):
    count = stats.shape[0]
    peak = jnp.max(stats, axis=0)
    scale = jnp.exp(stats - peak[None])
    rows = count * groups * 8
    flat = scale.reshape(rows, LANES)
    high = flat.astype(BF16)
    low = (flat - high.astype(F32)).astype(BF16)
    lift = spread_lanes(0).astype(BF16)
    scales = dot(high, lift) + dot(low, lift)
    sums = dot(
        stats.reshape(rows, LANES).astype(BF16), (spread_lanes(4) | spread_lanes(8)).astype(BF16)
    )
    numerator, denominator = [], []
    for g in range(groups):
        top, bottom = 0.0, 0.0
        for n in range(count):
            at = (n * groups + g) * 8
            factor = scales[at : at + 8]
            top = top + parts(n, g) * factor
            bottom = bottom + sums[at : at + 8] * factor
        numerator.append(top)
        denominator.append(bottom)
    return numerator, denominator, peak


def merge_kernel(
    in_ref, weight_ref, first_gain_ref, second_gain_ref, out_ref, gains_ref
):
    gains_ref[0, :] = first_gain_ref[...].astype(F32)
    gains_ref[1, :] = second_gain_ref[...].astype(F32)
    wide = HEADS_ROW * HD
    copies = out_ref.shape[0]
    stats = in_ref[:, :, wide:].astype(F32)[:, None]
    numerator, denominator, peak = merged(
        lambda n, g: in_ref[n, :, :wide].astype(F32), stats, 1
    )
    lane = iota((8, LANES), 1)
    packed = jnp.where(lane < HEADS_ROW, peak[0], 0.0)
    for j in range(HEADS_ROW):
        total = denominator[0][:, j * HD : (j + 1) * HD]
        high = total.astype(BF16).astype(F32)
        packed = jnp.where(lane == 4 + j, high, packed)
        packed = jnp.where(lane == 8 + j, total - high, packed)
    blocks = [numerator[0][:, j * HD : (j + 1) * HD] for j in range(HEADS_ROW)] + [packed]
    blocks = [block.astype(BF16) for block in blocks]
    for copy in range(copies):
        for j, block in enumerate(blocks):
            out_ref[copy, j * 8 : (j + 1) * 8, :] = block
        out_ref[copy, len(blocks) * 8 :, :] = weight_ref[:, copy * LANES : (copy + 1) * LANES]


def project_kernel(in_ref, residual_ref, router_ref, ids_ref, out_ref, stats_ref, weight_ref):
    requests = 4
    columns, groups = 4, 4
    head_rows = HEADS_ROW * 8
    weight_rows = in_ref.shape[1] - head_rows - 8
    sources = in_ref.shape[0]
    expert = expert_of_plane()
    for source in range(sources):
        place = source % columns * groups + source // columns
        stats_ref[place] = in_ref[source, head_rows : head_rows + 8, :].astype(F32)
        weight_ref[place * weight_rows : (place + 1) * weight_rows, :] = in_ref[
            source, head_rows + 8 :, :
        ]
    stats = stats_ref[...].reshape(columns, groups, 8, LANES)

    def part(n, g):
        source = g * columns + n
        return jnp.concatenate(
            [in_ref[source, j * 8 : (j + 1) * 8, :] for j in range(HEADS_ROW)], axis=1
        ).astype(F32)

    numerator, denominator, _ = merged(part, stats, groups)
    inputs = residual_ref[0].astype(F32)
    normed = (inputs * rms(inputs)).astype(BF16)
    logits = lax.dot_general(router_ref[...], normed, NT, preferred_element_type=F32)
    row = iota((8 * groups, 1), 0)
    gate = share_column(logits, ids_ref, expert, row // 8 * requests + row % requests)
    attended = jnp.concatenate(
        [top / jnp.maximum(bottom, 1e-30) for top, bottom in zip(numerator, denominator)], axis=0
    )
    gated = (attended.astype(BF16).astype(F32) * gate).astype(BF16)
    wide = HEADS_ROW * HD
    lower = dot(gated, weight_ref[:wide, :])
    upper = dot(gated, weight_ref[wide:, :])
    mixed = jnp.where(row % 8 < requests, lower, upper)
    sub = iota((8, LANES), 0)
    tiles = []
    for g in range(groups):
        tile = mixed[g * 8 : (g + 1) * 8]
        tiles.append(tile + pltpu.roll(tile, 4, 0))
    for pair in range(groups // 2):
        both = jnp.where(sub < requests, tiles[2 * pair], tiles[2 * pair + 1]).astype(BF16)
        for copy in range(out_ref.shape[0]):
            out_ref[copy, pair * 8 : (pair + 1) * 8, :] = both


def fold_kernel(in_ref, out_ref):
    total = in_ref[0].astype(F32)
    for n in range(1, in_ref.shape[0]):
        total = total + in_ref[n].astype(F32)
    total = total.astype(BF16)
    for copy in range(out_ref.shape[0]):
        out_ref[copy] = total


def expert_kernel(
    in_ref, residual_ref, gain_ref, router_ref, ids_ref, gate_ref, up_ref, down_ref, out_ref
):
    chunks = in_ref.shape[0]
    requests = in_ref.shape[1]
    middle = jnp.concatenate(
        [
            residual_ref[0, :, chunk * LANES : (chunk + 1) * LANES].astype(F32)
            + in_ref[chunk].astype(F32)
            for chunk in range(chunks)
        ],
        axis=1,
    )
    inputs = (middle * rms(middle) * gain_ref[0:1, :]).astype(BF16)
    logits = lax.dot_general(router_ref[...], inputs, NT, preferred_element_type=F32)
    share = share_column(logits, ids_ref, expert_of_plane(), iota((requests, 1), 0))
    gate = lax.dot_general(inputs, gate_ref[...], NT, preferred_element_type=F32)
    up = lax.dot_general(inputs, up_ref[...], NT, preferred_element_type=F32)
    hidden = (gate / (1.0 + jnp.exp(-gate)) * up * share).astype(BF16)
    out = dot(hidden, down_ref[...])
    for chunk in range(chunks):
        out_ref[chunk] = out[:, chunk * LANES : (chunk + 1) * LANES].astype(BF16)


def finish_kernel(in_ref, attention_ref, residual_ref, out_ref):
    total = attention_ref[0].astype(F32)
    for n in range(1, attention_ref.shape[0]):
        total = total + attention_ref[n].astype(F32)
    for n in range(in_ref.shape[0]):
        total = total + in_ref[n].astype(F32)
    chunk = lax.axis_index("req") * lax.axis_size("x") + lax.axis_index("x")
    at = pl.ds(pl.multiple_of(chunk * LANES, LANES), LANES)
    total = (total + residual_ref[0, :, at].astype(F32)).astype(out_ref.dtype)
    half = out_ref.shape[1]
    copies = out_ref.shape[0] // 2
    for stream in range(2):
        for copy in range(copies):
            out_ref[copy * 2 + stream] = total[stream * half : (stream + 1) * half]


def head_kernel(in_ref, gain_ref, words_ref, factor_ref, out_ref):
    half = in_ref.shape[1]
    chunks = in_ref.shape[0] // 2
    joined = jnp.concatenate(
        [
            jnp.concatenate(
                [in_ref[chunk * 2 + stream].astype(F32) for chunk in range(chunks)], axis=1
            )
            for stream in range(2)
        ],
        axis=0,
    )
    inputs = (joined * gain_ref[1:2, :]).astype(BF16)
    logits = lax.dot_general(inputs, words_ref[...], NT, preferred_element_type=F32)
    logits = logits * rms(joined)
    factor = factor_ref[:, :1]
    conditional, unconditional = logits[:half], logits[half:]
    out_ref[...] = unconditional + factor * (conditional - unconditional)


def exchanged(value, axis):
    return lax.all_to_all(value, axis, 0, 0, tiled=True)


def local(
    residual,
    queries,
    new_entries,
    key_cache,
    value_cache,
    lengths,
    attention_ids,
    expert_ids,
    attention_router,
    expert_router,
    attention_output,
    expert_gain,
    expert_gate,
    expert_up,
    expert_down,
    final_gain,
    unembedding,
    tenant_sizes,
    guidance,
):
    planes = lax.axis_size("z")
    plane = ("req", "x")
    members = lax.axis_size(plane)
    requests = residual.shape[1]
    shape = jax.ShapeDtypeStruct

    rows, positions = key_cache.shape[1:3]
    partial, factor, ids = call(
        attend_kernel,
        (
            shape((planes, 8, ROW), BF16),
            shape((requests // 2, LANES), F32),
            shape(expert_ids.shape[::-1], jnp.int32),
        ),
        [hbm()] * 9,
        [
            pltpu.VMEM(queries.shape, BF16),
            pltpu.VMEM((rows, positions + SPARE, D), BF16),
            pltpu.VMEM((rows, positions + SPARE, D), BF16),
            pltpu.VMEM(new_entries.shape, BF16),
            pltpu.SMEM(lengths.shape, jnp.int32),
            pltpu.SMEM(attention_ids.shape[::-1], jnp.int32),
            pltpu.SMEM(tenant_sizes.shape, jnp.int32),
            pltpu.SMEM(guidance.shape, jnp.int32),
            pltpu.VMEM((2, TOPK, 8, ROW), F32),
            pltpu.SemaphoreType.DMA((7,)),
            pltpu.SemaphoreType.DMA((2,)),
        ],
    )(
        *(
            pltpu.with_memory_space_constraint(operand, pltpu.HBM)
            for operand in (
                queries,
                key_cache,
                value_cache,
                new_entries,
                lengths,
                attention_ids.T,
                tenant_sizes,
                guidance,
                expert_ids.T,
            )
        )
    )
    partial = exchanged(partial, "z")

    weight_rows = attention_output.shape[0]
    merged_rows = HEADS_ROW * 8 + 8 + weight_rows
    both, gains = call(
        merge_kernel,
        (shape((members, merged_rows, LANES), BF16), shape((2, D), F32)),
        [vmem()] * 4,
    )(partial, attention_output, expert_gain, final_gain)
    both = exchanged(both, plane)

    chunk = shape((planes, requests, LANES), BF16)
    projected = call(
        project_kernel,
        chunk,
        [vmem()] * 4,
        [pltpu.VMEM((members, 8, LANES), F32), pltpu.VMEM((members * weight_rows, LANES), BF16)],
    )(both, residual, attention_router.T, attention_ids.T)
    projected = exchanged(projected, "z")

    spread = shape((members, requests, LANES), BF16)
    attention = call(fold_kernel, spread, [vmem()])(projected)
    attention = exchanged(attention, plane)

    hidden = call(expert_kernel, spread, [vmem()] * 8)(
        attention,
        residual,
        gains,
        expert_router.T,
        ids,
        expert_gate,
        expert_up,
        expert_down,
    )
    hidden = exchanged(hidden, plane)
    hidden = call(fold_kernel, chunk, [vmem()])(hidden)
    hidden = exchanged(hidden, "z")

    streams = lax.axis_size("cfg")
    final = call(
        finish_kernel, shape((streams * members, requests // 2, LANES), BF16), [vmem()] * 3
    )(hidden, projected, residual)
    final = exchanged(final, plane + ("cfg",))

    return call(
        head_kernel,
        shape((requests // 2, unembedding.shape[0]), F32),
        [vmem()] * 4,
    )(final, gains, unembedding, factor)


def solution(mesh):
    sizes = mesh.devices.shape
    split = Mesh(mesh.devices.reshape(sizes[0], 16, sizes[1] // 16, sizes[2]), ("cfg", "z", "x", "req"))
    blk = ("z", "x")
    rows = P(("z", "x", "req"), None)
    placed = (
        P("cfg", None, None),
        P("cfg", "req", None),
        P("cfg", "req", None, None),
        P("cfg", "req", blk, None),
        P("cfg", "req", blk, None),
        P("cfg", "req"),
        P(),
        P(),
        P(),
        P(),
        rows,
        P(),
        rows,
        rows,
        rows,
        P(),
        rows,
        P(),
        P(),
    )
    return jax.shard_map(
        local,
        mesh=split,
        in_specs=placed,
        out_specs=P("cfg", ("z", "x", "req")),
        check_vma=False,
    )
```

```python
import math

import jax
import jax.numpy as jnp
from jax import lax
from jax.experimental import pallas as pl
from jax.experimental.pallas import tpu as pltpu
from jax.sharding import Mesh
from jax.sharding import PartitionSpec as P

D = 2048
H = 16
HD = 128
FF = 5632
TOPK = 2
EPS = 1e-05
NEG = -1e30
SPARE = 16
LANES = 128
HEADS_ROW = 4
ROW = HEADS_ROW * HD + LANES
SCALE = 1.0 / math.sqrt(HD)

F32 = jnp.float32
BF16 = jnp.bfloat16
NT = (((1,), (1,)), ((), ()))


def vmem():
    return pl.BlockSpec(memory_space=pltpu.VMEM)


def hbm():
    return pl.BlockSpec(memory_space=pltpu.HBM)


def call(body, outs, specs, scratch=()):
    return pl.pallas_call(
        body,
        out_shape=outs,
        in_specs=specs,
        out_specs=jax.tree.map(lambda _: vmem(), outs),
        scratch_shapes=list(scratch),
        compiler_params=pltpu.CompilerParams(vmem_limit_bytes=48 * 1024 * 1024),
    )


def iota(shape, dim):
    return lax.broadcasted_iota(jnp.int32, shape, dim)


def dot(a, b):
    return jnp.dot(a, b, preferred_element_type=F32)


def rms(values):
    return lax.rsqrt(jnp.mean(values * values, axis=-1, keepdims=True) + EPS)


def expert_of_plane():
    return lax.axis_index("z") // 2


def share_column(logits_t, ids_ref, expert, lane_of_row):
    experts = iota(logits_t.shape, 0)
    first_id, second_id = ids_ref[0:1, :], ids_ref[1:2, :]
    first = jnp.sum(jnp.where(experts == first_id, logits_t, 0.0), axis=0, keepdims=True)
    second = jnp.sum(jnp.where(experts == second_id, logits_t, 0.0), axis=0, keepdims=True)
    gate_first = 1.0 / (1.0 + jnp.exp(second - first))
    gate_second = 1.0 / (1.0 + jnp.exp(first - second))
    share = jnp.where(first_id == expert, gate_first, 0.0) + jnp.where(
        second_id == expert, gate_second, 0.0
    )
    lanes = iota((lane_of_row.shape[0], share.shape[1]), 1)
    return jnp.sum(jnp.where(lanes == lane_of_row, share, 0.0), axis=1, keepdims=True)


def guidance_factor(sizes_ref, guidance_ref, half):
    request = lax.axis_index("cfg") * half + iota((half, 1), 0)
    tenants = sizes_ref.shape[0]
    tenant = jnp.zeros((half, 1), jnp.int32)
    end = 0
    for t in range(tenants):
        end = end + sizes_ref[t]
        tenant = tenant + (request >= end).astype(jnp.int32)
    chosen = jnp.zeros((half, 1), jnp.int32)
    for t in range(tenants):
        chosen = jnp.where(tenant == t, guidance_ref[t], chosen)
    return chosen.astype(F32) / 4.0


def attend_kernel(
    q_hbm,
    k_hbm,
    v_hbm,
    new_hbm,
    lengths_hbm,
    ids_hbm,
    sizes_hbm,
    guidance_hbm,
    expert_ids_hbm,
    out_ref,
    factor_ref,
    expert_ids_ref,
    q_ref,
    k_ref,
    v_ref,
    new_ref,
    lengths_ref,
    ids_ref,
    sizes_ref,
    guidance_ref,
    rows_ref,
    small_sems,
    cache_sems,
):
    requests, positions = k_hbm.shape[1], k_hbm.shape[2]
    small = [
        pltpu.make_async_copy(source, target, small_sems.at[n])
        for n, (source, target) in enumerate(
            [
                (q_hbm, q_ref),
                (new_hbm, new_ref),
                (lengths_hbm, lengths_ref),
                (ids_hbm, ids_ref),
                (sizes_hbm, sizes_ref),
                (guidance_hbm, guidance_ref),
                (expert_ids_hbm, expert_ids_ref),
            ]
        )
    ]
    keys = pltpu.make_async_copy(k_hbm.at[0], k_ref.at[:, :positions], cache_sems.at[0])
    values_in = pltpu.make_async_copy(v_hbm.at[0], v_ref.at[:, :positions], cache_sems.at[1])
    keys.start()
    values_in.start()
    for copy in small:
        copy.start()
    block = lax.axis_index("z") * lax.axis_size("x") + lax.axis_index("x")
    owner = block == 0
    first_request = lax.axis_index("req") * requests
    own_head = iota((H, D), 0) == iota((H, D), 1) // HD
    for copy in [*small, keys, values_in]:
        copy.wait()
    queries = q_ref[0].astype(F32)
    wide = [
        jnp.concatenate(
            [
                jnp.where(own_head, queries[r : r + 1, k * D : (k + 1) * D], 0.0)
                for k in range(TOPK)
            ],
            axis=0,
        ).astype(BF16)
        for r in range(requests)
    ]
    new_row = (iota((SPARE, D), 0) == 0) & owner
    for r in range(requests):
        entry = new_ref[0, r].astype(F32)
        k_ref[r, positions:, :] = jnp.where(new_row, entry[0:1, :], 0.0).astype(BF16)
        v_ref[r, positions:, :] = jnp.where(new_row, entry[1:2, :], 0.0).astype(BF16)
    factor_ref[...] = jnp.broadcast_to(
        guidance_factor(sizes_ref, guidance_ref, factor_ref.shape[0]), factor_ref.shape
    )
    scores = jnp.concatenate(
        [
            lax.dot_general(wide[r], k_ref[r], NT, preferred_element_type=F32)
            for r in range(requests)
        ],
        axis=0,
    )
    scores = scores * SCALE
    heads = TOPK * H
    request_of_row = iota((requests * heads, 1), 0) // heads
    length = jnp.zeros((requests * heads, 1), jnp.int32)
    for r in range(requests):
        length = jnp.where(request_of_row == r, lengths_ref[0, r], length)
    column = iota(scores.shape, 1)
    live = (column < positions) & (block * positions + column < length)
    live = live | ((column == positions) & owner)
    top = jnp.max(jnp.where(live, scores, NEG), axis=1, keepdims=True)
    peaks = top.astype(BF16).astype(F32)
    weights = jnp.where(live, jnp.exp(scores - peaks), 0.0)
    totals = jnp.sum(weights, axis=1, keepdims=True)
    highs = totals.astype(BF16).astype(F32)
    lows = totals - highs
    weights = weights.astype(BF16)
    products = [dot(weights[r * heads : (r + 1) * heads], v_ref[r]) for r in range(requests)]
    sub = iota((8, LANES), 0)
    lane = iota((8, LANES), 1)
    for r in range(requests):
        at = slice(r * heads, (r + 1) * heads)
        values, peak, high, low = products[r], peaks[at], highs[at], lows[at]
        for k in range(TOPK):
            for quarter in range(H // HEADS_ROW):
                half, group = quarter // 2, quarter % 2
                base = k * H + (quarter // 2) * 8
                parts = []
                for j in range(HEADS_ROW):
                    head = quarter * HEADS_ROW + j
                    tile = values[base : base + 8, head * HD : (head + 1) * HD]
                    parts.append(jnp.sum(jnp.where(sub == head % 8, tile, 0.0), axis=0, keepdims=True))
                part = sub - group * HEADS_ROW
                here = (part >= 0) & (part < HEADS_ROW)
                stats = jnp.where(lane == part, peak[base : base + 8], 0.0)
                stats = stats + jnp.where(lane == part + 4, high[base : base + 8], 0.0)
                stats = stats + jnp.where(lane == part + 8, low[base : base + 8], 0.0)
                parts.append(jnp.sum(jnp.where(here, stats, 0.0), axis=0, keepdims=True))
                row = group * requests + r
                rows_ref[half, k, row : row + 1, :] = jnp.concatenate(parts, axis=1)
    request = iota((8, 1), 0) % requests
    chosen = []
    for k in range(TOPK):
        picked = jnp.zeros((8, 1), jnp.int32)
        for r in range(requests):
            picked = jnp.where(request == r, ids_ref[k, first_request + r], picked)
        chosen.append(picked)
    for plane in range(out_ref.shape[0]):
        expert, half = plane // 2, plane % 2
        message = jnp.where(chosen[0] == expert, rows_ref[half, 0], 0.0)
        message = message + jnp.where(chosen[1] == expert, rows_ref[half, 1], 0.0)
        out_ref[plane] = message.astype(BF16)


def spread_lanes(first_lane):
    rows, columns = iota((LANES, HEADS_ROW * HD), 0), iota((LANES, HEADS_ROW * HD), 1)
    return rows == first_lane + columns // HD


def merged(parts, stats, groups):
    count = stats.shape[0]
    peak = jnp.max(stats, axis=0)
    scale = jnp.exp(stats - peak[None])
    rows = count * groups * 8
    flat = scale.reshape(rows, LANES)
    high = flat.astype(BF16)
    low = (flat - high.astype(F32)).astype(BF16)
    lift = spread_lanes(0).astype(BF16)
    scales = dot(high, lift) + dot(low, lift)
    sums = dot(
        stats.reshape(rows, LANES).astype(BF16), (spread_lanes(4) | spread_lanes(8)).astype(BF16)
    )
    numerator, denominator = [], []
    for g in range(groups):
        top, bottom = 0.0, 0.0
        for n in range(count):
            at = (n * groups + g) * 8
            factor = scales[at : at + 8]
            top = top + parts(n, g) * factor
            bottom = bottom + sums[at : at + 8] * factor
        numerator.append(top)
        denominator.append(bottom)
    return numerator, denominator, peak


def merge_kernel(
    in_ref, weight_ref, first_gain_ref, second_gain_ref, out_ref, gains_ref
):
    gains_ref[0, :] = first_gain_ref[...].astype(F32)
    gains_ref[1, :] = second_gain_ref[...].astype(F32)
    wide = HEADS_ROW * HD
    copies = out_ref.shape[0]
    stats = in_ref[:, :, wide:].astype(F32)[:, None]
    numerator, denominator, peak = merged(
        lambda n, g: in_ref[n, :, :wide].astype(F32), stats, 1
    )
    lane = iota((8, LANES), 1)
    packed = jnp.where(lane < HEADS_ROW, peak[0], 0.0)
    for j in range(HEADS_ROW):
        total = denominator[0][:, j * HD : (j + 1) * HD]
        high = total.astype(BF16).astype(F32)
        packed = jnp.where(lane == 4 + j, high, packed)
        packed = jnp.where(lane == 8 + j, total - high, packed)
    blocks = [numerator[0][:, j * HD : (j + 1) * HD] for j in range(HEADS_ROW)] + [packed]
    blocks = [block.astype(BF16) for block in blocks]
    for copy in range(copies):
        for j, block in enumerate(blocks):
            out_ref[copy, j * 8 : (j + 1) * 8, :] = block
        out_ref[copy, len(blocks) * 8 :, :] = weight_ref[:, copy * LANES : (copy + 1) * LANES]


def project_kernel(in_ref, residual_ref, router_ref, ids_ref, out_ref, stats_ref, weight_ref):
    requests = 4
    columns, groups = 4, 4
    head_rows = HEADS_ROW * 8
    weight_rows = in_ref.shape[1] - head_rows - 8
    sources = in_ref.shape[0]
    expert = expert_of_plane()
    for source in range(sources):
        place = source % columns * groups + source // columns
        stats_ref[place] = in_ref[source, head_rows : head_rows + 8, :].astype(F32)
        weight_ref[place * weight_rows : (place + 1) * weight_rows, :] = in_ref[
            source, head_rows + 8 :, :
        ]
    stats = stats_ref[...].reshape(columns, groups, 8, LANES)

    def part(n, g):
        source = g * columns + n
        return jnp.concatenate(
            [in_ref[source, j * 8 : (j + 1) * 8, :] for j in range(HEADS_ROW)], axis=1
        ).astype(F32)

    numerator, denominator, _ = merged(part, stats, groups)
    inputs = residual_ref[0].astype(F32)
    normed = (inputs * rms(inputs)).astype(BF16)
    logits = lax.dot_general(router_ref[...], normed, NT, preferred_element_type=F32)
    row = iota((8 * groups, 1), 0)
    gate = share_column(logits, ids_ref, expert, row // 8 * requests + row % requests)
    attended = jnp.concatenate(
        [top / jnp.maximum(bottom, 1e-30) for top, bottom in zip(numerator, denominator)], axis=0
    )
    gated = (attended.astype(BF16).astype(F32) * gate).astype(BF16).astype(F32)
    low_heads = row % 8 < requests
    none = jnp.zeros_like(gated)
    both_halves = jnp.concatenate(
        [jnp.where(low_heads, gated, none), jnp.where(low_heads, none, gated)], axis=1
    )
    mixed = dot(both_halves.astype(BF16), weight_ref[...])
    sub = iota((8, LANES), 0)
    tiles = []
    for g in range(groups):
        tile = mixed[g * 8 : (g + 1) * 8]
        tiles.append(tile + pltpu.roll(tile, 4, 0))
    for pair in range(groups // 2):
        both = jnp.where(sub < requests, tiles[2 * pair], tiles[2 * pair + 1]).astype(BF16)
        for copy in range(out_ref.shape[0]):
            out_ref[copy, pair * 8 : (pair + 1) * 8, :] = both


def fold_kernel(in_ref, out_ref):
    total = in_ref[0].astype(F32)
    for n in range(1, in_ref.shape[0]):
        total = total + in_ref[n].astype(F32)
    total = total.astype(BF16)
    for copy in range(out_ref.shape[0]):
        out_ref[copy] = total


def expert_kernel(
    in_ref, residual_ref, gain_ref, router_ref, ids_ref, gate_ref, up_ref, down_ref, out_ref
):
    chunks = in_ref.shape[0]
    requests = in_ref.shape[1]
    middle = jnp.concatenate(
        [
            residual_ref[0, :, chunk * LANES : (chunk + 1) * LANES].astype(F32)
            + in_ref[chunk].astype(F32)
            for chunk in range(chunks)
        ],
        axis=1,
    )
    inputs = (middle * rms(middle) * gain_ref[0:1, :]).astype(BF16)
    logits = lax.dot_general(router_ref[...], inputs, NT, preferred_element_type=F32)
    share = share_column(logits, ids_ref, expert_of_plane(), iota((requests, 1), 0))
    gate = lax.dot_general(inputs, gate_ref[...], NT, preferred_element_type=F32)
    up = lax.dot_general(inputs, up_ref[...], NT, preferred_element_type=F32)
    hidden = (gate / (1.0 + jnp.exp(-gate)) * up * share).astype(BF16)
    out = dot(hidden, down_ref[...])
    for chunk in range(chunks):
        out_ref[chunk] = out[:, chunk * LANES : (chunk + 1) * LANES].astype(BF16)


def finish_kernel(in_ref, attention_ref, residual_ref, out_ref):
    total = attention_ref[0].astype(F32)
    for n in range(1, attention_ref.shape[0]):
        total = total + attention_ref[n].astype(F32)
    for n in range(in_ref.shape[0]):
        total = total + in_ref[n].astype(F32)
    chunk = lax.axis_index("req") * lax.axis_size("x") + lax.axis_index("x")
    at = pl.ds(pl.multiple_of(chunk * LANES, LANES), LANES)
    total = (total + residual_ref[0, :, at].astype(F32)).astype(out_ref.dtype)
    half = out_ref.shape[1]
    copies = out_ref.shape[0] // 2
    for stream in range(2):
        for copy in range(copies):
            out_ref[copy * 2 + stream] = total[stream * half : (stream + 1) * half]


def head_kernel(in_ref, gain_ref, words_ref, factor_ref, out_ref):
    half = in_ref.shape[1]
    chunks = in_ref.shape[0] // 2
    joined = jnp.concatenate(
        [
            jnp.concatenate(
                [in_ref[chunk * 2 + stream].astype(F32) for chunk in range(chunks)], axis=1
            )
            for stream in range(2)
        ],
        axis=0,
    )
    inputs = (joined * gain_ref[1:2, :]).astype(BF16)
    logits = lax.dot_general(inputs, words_ref[...], NT, preferred_element_type=F32)
    logits = logits * rms(joined)
    factor = factor_ref[:, :1]
    conditional, unconditional = logits[:half], logits[half:]
    out_ref[...] = unconditional + factor * (conditional - unconditional)


def exchanged(value, axis):
    return lax.all_to_all(value, axis, 0, 0, tiled=True)


def local(
    residual,
    queries,
    new_entries,
    key_cache,
    value_cache,
    lengths,
    attention_ids,
    expert_ids,
    attention_router,
    expert_router,
    attention_output,
    expert_gain,
    expert_gate,
    expert_up,
    expert_down,
    final_gain,
    unembedding,
    tenant_sizes,
    guidance,
):
    planes = lax.axis_size("z")
    plane = ("req", "x")
    members = lax.axis_size(plane)
    requests = residual.shape[1]
    shape = jax.ShapeDtypeStruct

    rows, positions = key_cache.shape[1:3]
    partial, factor, ids = call(
        attend_kernel,
        (
            shape((planes, 8, ROW), BF16),
            shape((requests // 2, LANES), F32),
            shape(expert_ids.shape[::-1], jnp.int32),
        ),
        [hbm()] * 9,
        [
            pltpu.VMEM(queries.shape, BF16),
            pltpu.VMEM((rows, positions + SPARE, D), BF16),
            pltpu.VMEM((rows, positions + SPARE, D), BF16),
            pltpu.VMEM(new_entries.shape, BF16),
            pltpu.SMEM(lengths.shape, jnp.int32),
            pltpu.SMEM(attention_ids.shape[::-1], jnp.int32),
            pltpu.SMEM(tenant_sizes.shape, jnp.int32),
            pltpu.SMEM(guidance.shape, jnp.int32),
            pltpu.VMEM((2, TOPK, 8, ROW), F32),
            pltpu.SemaphoreType.DMA((7,)),
            pltpu.SemaphoreType.DMA((2,)),
        ],
    )(
        *(
            pltpu.with_memory_space_constraint(operand, pltpu.HBM)
            for operand in (
                queries,
                key_cache,
                value_cache,
                new_entries,
                lengths,
                attention_ids.T,
                tenant_sizes,
                guidance,
                expert_ids.T,
            )
        )
    )
    partial = exchanged(partial, "z")

    weight_rows = attention_output.shape[0]
    merged_rows = HEADS_ROW * 8 + 8 + weight_rows
    both, gains = call(
        merge_kernel,
        (shape((members, merged_rows, LANES), BF16), shape((2, D), F32)),
        [vmem()] * 4,
    )(partial, attention_output, expert_gain, final_gain)
    both = exchanged(both, plane)

    chunk = shape((planes, requests, LANES), BF16)
    projected = call(
        project_kernel,
        chunk,
        [vmem()] * 4,
        [pltpu.VMEM((members, 8, LANES), F32), pltpu.VMEM((members * weight_rows, LANES), BF16)],
    )(both, residual, attention_router.T, attention_ids.T)
    projected = exchanged(projected, "z")

    spread = shape((members, requests, LANES), BF16)
    attention = call(fold_kernel, spread, [vmem()])(projected)
    attention = exchanged(attention, plane)

    hidden = call(expert_kernel, spread, [vmem()] * 8)(
        attention,
        residual,
        gains,
        expert_router.T,
        ids,
        expert_gate,
        expert_up,
        expert_down,
    )
    hidden = exchanged(hidden, plane)
    hidden = call(fold_kernel, chunk, [vmem()])(hidden)
    hidden = exchanged(hidden, "z")

    streams = lax.axis_size("cfg")
    final = call(
        finish_kernel, shape((streams * members, requests // 2, LANES), BF16), [vmem()] * 3
    )(hidden, projected, residual)
    final = exchanged(final, plane + ("cfg",))

    return call(
        head_kernel,
        shape((requests // 2, unembedding.shape[0]), F32),
        [vmem()] * 4,
    )(final, gains, unembedding, factor)


def solution(mesh):
    sizes = mesh.devices.shape
    split = Mesh(mesh.devices.reshape(sizes[0], 16, sizes[1] // 16, sizes[2]), ("cfg", "z", "x", "req"))
    blk = ("z", "x")
    rows = P(("z", "x", "req"), None)
    placed = (
        P("cfg", None, None),
        P("cfg", "req", None),
        P("cfg", "req", None, None),
        P("cfg", "req", blk, None),
        P("cfg", "req", blk, None),
        P("cfg", "req"),
        P(),
        P(),
        P(),
        P(),
        rows,
        P(),
        rows,
        rows,
        rows,
        P(),
        rows,
        P(),
        P(),
    )
    return jax.shard_map(
        local,
        mesh=split,
        in_specs=placed,
        out_specs=P("cfg", ("z", "x", "req")),
        check_vma=False,
    )
```
